128 devices in a mesh: space: 16 (over x, z), mem: 8 (over y, core).
Axes of the slice: x: 4, y: 4, z: 4, core: 2. Of those that a mesh axis runs over, the one named last changes fastest.
Arguments:
- ensemble_state: bfloat16 [256, 1024, 256], P('mem', 'space'), may hold values from -6 to 6
- obs_ens: bfloat16 [256, 1024, 128], P('mem', 'space'), may hold values from -6 to 6
- innovation: float32 [1024, 128], P('space'), may hold values from -6 to 6
- obs_prec: float32 [1024, 128], P('space'), may hold values from 0.25 to 2
- block_list: int32 [1024, 8], P('space'), may hold values from 0 to 1023, as said below
- block_count: int32 [1024], P('space'), may hold values from 1 to 8
- loc_weight: float32 [1024, 8], P('space'), may hold values from 0.1 to 1
- prior_weight: float32 [1024, 256], P('space'), may hold values from 0.1 to 10, as said below
Outputs:
- analysis: bfloat16 [256, 1024, 256], P('mem', 'space')
The draws below stay inside these ranges and needn't reach their ends.
Inputs may be any that keep to these rules, and one draw needn't show every extreme that they name: `block_list`: among the 64 entries of the regions r with the same r // 8, at most 6 name blocks b with the same b // 64, and exactly 6 do for one such value. `prior_weight`: Positive.
All inputs are finite; a program needn't handle non-finite values.
Results may differ from the reference program's by a relative error of at most 0.012.
Values may be sent and summed in bfloat16 or wider, within the bound.
A program may use at most 128 MiB of HBM per device.

```python
import math
import jax
import jax.numpy as jnp
from jax import lax

K = 256
P_SIZE = 256
OB = 128
L = 8
REGIONS = 1024
BLK_DEV = 64
NBLK = 1024
GROUP_REG = 8
N_SPACE = 16


def draw_block_list(key, part):
    groups = REGIONS // GROUP_REG
    entries = GROUP_REG * L
    mean_load = entries // N_SPACE

    def one_group(group_key):
        sub_keys = jax.random.split(group_key, 3)
        hot_target = jax.random.randint(sub_keys[0], (), 0, N_SPACE)
        positions = jnp.arange(entries, dtype=jnp.int32)
        base_target = positions % N_SPACE
        cold_target = (hot_target + 1) % N_SPACE
        moved_entries = (base_target == cold_target) & (positions // N_SPACE < mean_load // 2)
        target = jnp.where(moved_entries, hot_target, base_target)
        target = jax.random.permutation(sub_keys[1], target)
        local_ids = jax.random.randint(sub_keys[2], (entries,), 0, BLK_DEV)
        return (target * BLK_DEV + local_ids).reshape(GROUP_REG, L)
    drawn = jax.vmap(one_group)(jax.random.split(key, groups))
    return drawn.reshape(REGIONS, L).astype(jnp.int32)


def draw_block_count(key, part):
    counts = jax.random.randint(key, (REGIONS,), 1, L + 1)
    return counts.at[0].set(L).at[1].set(1).astype(jnp.int32)


def draw_prior_weight(key, part):
    ramp = jnp.arange(K, dtype=jnp.float32) / (K - 1.0)
    rising = jnp.exp(jnp.log(3.0) * ramp)
    noise = jnp.exp(jax.random.uniform(key, (REGIONS, K), jnp.float32, -0.69, 0.69))
    return (rising[None, :] * noise).astype(jnp.float32)


def block_levels(rng, extent, pieces, low, high):
    loudness = 1.0
    for dim, parts in pieces:
        heights = jax.random.uniform(jax.random.fold_in(jax.random.fold_in(rng, 6), dim), (parts,), jnp.float32, low / len(pieces), high / len(pieces))
        loudness = loudness * jnp.repeat(jnp.exp(heights), extent[dim] // parts).reshape((-1,) + (1,) * (len(extent) - 1 - dim))
    return loudness


def bell_draw(own_key, dims, scale, reach, cuts=(), kind=jnp.bfloat16):
    level = block_levels(own_key, dims, cuts, -0.22, 0.18) if cuts else 1.0
    values = jax.random.normal(own_key, dims, jnp.float32) * scale * level
    return jnp.minimum(jnp.maximum(values, -reach), reach).astype(kind)


def setup_inputs(seed: int = 0) -> dict:
    streams_of = jax.random.split(jax.random.key(seed), 9)
    ensemble_state = bell_draw(streams_of[0], (K, REGIONS, P_SIZE), 1.0, 6.0, ((0, 8), (1, 16)))
    obs_ens = bell_draw(streams_of[1], (K, NBLK, OB), 1.0, 6.0, ((0, 8), (1, 16)))
    innovation = bell_draw(streams_of[2], (NBLK, OB), 1.0, 6.0, ((0, 16),), jnp.float32)
    obs_prec = jnp.clip(jnp.exp(math.log(2.0) - 2.0794415 * jax.random.uniform(streams_of[3], (NBLK, OB), jnp.float32) ** block_levels(streams_of[3], (NBLK, OB), ((0, 16),), -0.2, 0.2)), 0.25, 2.0)
    block_list = draw_block_list(jax.random.fold_in(streams_of[8], 71), 0)
    block_count = draw_block_count(jax.random.fold_in(streams_of[8], 71), 0)
    loc_weight = jnp.clip(jnp.exp(math.log(1.0) - 2.3025851 * jax.random.uniform(streams_of[6], (REGIONS, L), jnp.float32) ** block_levels(streams_of[6], (REGIONS, L), ((0, 16),), -0.2, 0.2)), 0.1, 1.0)
    prior_weight = draw_prior_weight(jax.random.fold_in(streams_of[8], 71), 0)
    return {"ensemble_state": ensemble_state, "obs_ens": obs_ens, "innovation": innovation, "obs_prec": obs_prec, "block_list": block_list, "block_count": block_count, "loc_weight": loc_weight, "prior_weight": prior_weight}


INFLATION = 1.1

def transform(gram_blocks, projection, prior_rows):
    highest = lax.Precision.HIGHEST
    members = gram_blocks.shape[-1]
    shares = prior_rows / lax.optimization_barrier(jnp.sum(prior_rows, axis=1, keepdims=True))
    root_q = jnp.sqrt(members * shares)
    left_term = jnp.einsum('rk,rkj->rj', shares, gram_blocks, precision=highest)
    centred = gram_blocks - left_term[:, None, :]
    right_term = jnp.einsum('rik,rk->ri', centred, shares, precision=highest)
    centred = centred - right_term[:, :, None]
    identity = jnp.eye(members, dtype=jnp.float32)
    system = root_q[:, :, None] * centred * root_q[:, None, :] + (members - 1) / INFLATION * identity
    vector = root_q * (projection - lax.optimization_barrier(jnp.sum(shares * projection, axis=1, keepdims=True)))
    factor = jnp.linalg.cholesky(system)
    inverse = jax.scipy.linalg.solve_triangular(factor, jnp.broadcast_to(identity, system.shape), lower=True)
    solved = jnp.einsum('rij,rj->ri', inverse, vector, precision=highest)
    weights = jnp.einsum('rji,rj->ri', inverse, solved, precision=highest)
    spread = jnp.sqrt(members - 1.0) * jnp.transpose(inverse, (0, 2, 1))
    mixing = root_q[:, :, None] * (weights[:, :, None] + spread)
    mixing = mixing - shares[:, :, None] * lax.optimization_barrier(jnp.sum(mixing, axis=1, keepdims=True)) + shares[:, :, None]
    return mixing

def reference(ensemble_state, obs_ens, innovation, obs_prec, block_list, block_count, loc_weight, prior_weight):
    highest = lax.Precision.HIGHEST
    batch_regions = 16

    def one_batch(first_row):
        block_ids = lax.dynamic_slice_in_dim(block_list, first_row, batch_regions, 0)
        counts = lax.dynamic_slice_in_dim(block_count, first_row, batch_regions, 0)
        loc_rows = lax.dynamic_slice_in_dim(loc_weight, first_row, batch_regions, 0)
        prior_rows = lax.dynamic_slice_in_dim(prior_weight, first_row, batch_regions, 0)
        active = (jnp.arange(L, dtype=jnp.int32)[None, :] < counts[:, None]).astype(jnp.float32)
        obs_weight = (active * loc_rows)[:, :, None] * obs_prec[block_ids]
        obs_scale = jnp.sqrt(obs_weight)
        picked = obs_ens[:, block_ids, :].astype(jnp.float32)
        scaled = (picked * obs_scale[None]).astype(jnp.bfloat16).astype(jnp.float32)
        gram_blocks = jnp.einsum('krlo,jrlo->rkj', scaled, scaled, precision=highest)
        projection = jnp.einsum('krlo,rlo->rk', scaled, obs_scale * innovation[block_ids], precision=highest)
        mixing = transform(gram_blocks, projection, prior_rows)
        states = lax.dynamic_slice_in_dim(ensemble_state, first_row, batch_regions, 1).astype(jnp.float32)
        return jnp.einsum('krp,rkj->jrp', states, mixing, precision=highest).astype(jnp.bfloat16)
    batch_starts = jnp.arange(REGIONS // batch_regions, dtype=jnp.int32) * batch_regions
    results = lax.map(one_batch, batch_starts)
    return jnp.transpose(results, (1, 0, 2, 3)).reshape(K, REGIONS, P_SIZE)
```

```python
import functools
import math

import jax
import jax.numpy as jnp
from jax import lax
from jax.experimental import pallas as pl
from jax.experimental.pallas import tpu as pltpu
from jax.sharding import PartitionSpec as P

INFLATION = 1.1
HIGHEST = lax.Precision.HIGHEST
F32 = jnp.float32
BF16 = jnp.bfloat16


def dot(a, b, dims, precision=None):
    return lax.dot_general(a, b, (dims, ((), ())), precision=precision, preferred_element_type=F32)


def split(x):
    high = x.astype(BF16)
    return high, (x - high.astype(F32)).astype(BF16)


def dot_f32(a, b, dims, mode):
    if mode == 6:
        return dot(a, b, dims, HIGHEST)
    ah, al = split(a)
    bh, bl = split(b)
    return dot(ah, bh, dims) + (dot(ah, bl, dims) + dot(al, bh, dims))


def eliminate(rows, group):
    count = len(rows)
    rows = list(rows)

    def lane(x, i):
        return jnp.broadcast_to(x[:, i : i + 1], x.shape)

    for k in range(0, count, group):
        small = {(a, b): lane(rows[k + a], k + b) for a in range(group) for b in range(a, group)}
        for a in range(group):
            root = lax.rsqrt(small[a, a])
            upper = {b: small[a, b] * root for b in range(a + 1, group)}
            rows[k + a] = rows[k + a] * root
            for c in range(a + 1, group):
                rows[k + c] = rows[k + c] - upper[c] * rows[k + a]
                for b in range(c, group):
                    small[c, b] = small[c, b] - upper[c] * upper[b]
        for i in range(k + group, count):
            for a in range(group):
                rows[i] = rows[i] - lane(rows[k + a], i) * rows[k + a]
    return rows


def analyse(
    me, list_ref, count_ref, loc_ref, table_ref, prior_ref, obs_ref, state_ref, out_ref,
    seen, extra, system, diag, inv, qcol, *, nb, group, mode,
):
    mems, entries, members_dev, width = obs_ref.shape
    members = mems * members_dev
    slots = list_ref.shape[1]
    regions = entries // slots
    first = me * regions
    shares_all = prior_ref[pl.ds(first, regions), :]
    shares_all = shares_all / jnp.sum(shares_all, axis=1, keepdims=True)
    root_all = jnp.sqrt(members * shares_all)
    root_t = jnp.transpose(root_all)
    for r in range(regions):
        qcol[r] = jnp.broadcast_to(root_t[:, r : r + 1], (members, 128))
    extra[...] = jnp.zeros_like(extra)
    row_id = lax.broadcasted_iota(jnp.int32, (members, members), 0)
    col_id = lax.broadcasted_iota(jnp.int32, (members, members), 1)
    vec_scr = []

    def shares_of(r):
        s = prior_ref[pl.ds(first + r, 1), :]
        return s / jnp.sum(s, axis=1, keepdims=True)

    def build(r, carry):
        row = first + r
        for l in range(slots):
            block = list_ref[row, l]
            both = table_ref[pl.ds(block, 1), :]
            live = jnp.where(l < count_ref[row], loc_ref[row, l], 0.0)
            scale = jnp.sqrt(live * both[:, :width])
            picked = obs_ref[:, r * slots + l].reshape(members, width).astype(F32)
            cols = slice(l * width, (l + 1) * width)
            seen[:, cols] = (picked * scale).astype(BF16)
            high, low = split(scale * both[:, width:])
            extra[0:1, cols] = high.astype(F32)
            extra[1:2, cols] = low.astype(F32)
        all_seen = seen[...]
        gram = dot(all_seen, all_seen, ((1,), (1,)))
        proj = dot(extra[...].astype(BF16), all_seen, ((1,), (1,)))
        proj = proj[0:1] + proj[1:2]
        shares = shares_of(r)
        root = jnp.sqrt(members * shares)
        left = dot(jnp.broadcast_to(shares, (8, members)), gram, ((1,), (0,)), HIGHEST)[0:1]
        centred = gram - left
        centred = centred - jnp.sum(centred * shares, axis=1, keepdims=True)
        q = jnp.concatenate([qcol[r]] * (members // 128), axis=1)
        full = q * centred * root + jnp.where(row_id == col_id, (members - 1) / INFLATION, 0.0)
        at = pl.ds(pl.multiple_of(r * members, members), members)
        for half in range(members // 128):
            system[half, at, :] = full[:, half * 128 : (half + 1) * 128]
        vector = root * (proj - jnp.sum(shares * proj, axis=1, keepdims=True))
        inv[pl.ds(r, 1), :] = vector
        return carry

    lax.fori_loop(0, regions, build, 0)

    lane_id = lax.broadcasted_iota(jnp.int32, (regions, 128), 1)
    halves = members // 128
    per_half = 128 // nb
    for b in range(members // nb):
        half, place = b // per_half, (b % per_half) * nb
        def factor(_, carry):
            rows = []
            for i in range(nb):
                x = system[half, pl.ds(b * nb + i, regions, stride=members), :]
                if place:
                    x = pltpu.roll(x, 128 - place, 1)
                rows.append(jnp.where(lane_id < nb, x, jnp.where(lane_id == nb + i, 1.0, 0.0)))
            rows = eliminate(rows, group)
            for i in range(nb):
                diag[pl.ds(i, regions, stride=nb), :] = rows[i]
            return carry

        factor(0, 0)

        def sweep(r, carry):
            start = r * members + b * nb
            here = pl.ds(pl.multiple_of(start, nb), nb)
            small = diag[pl.ds(pl.multiple_of(r * nb, nb), nb), :][:, nb : 2 * nb]
            band = jnp.concatenate([system[h, here, :] for h in range(halves)], axis=1)
            ids = lax.broadcasted_iota(jnp.int32, (nb, members), 1)
            rid = lax.broadcasted_iota(jnp.int32, (nb, members), 0)
            mine = (ids >= b * nb) & (ids < (b + 1) * nb)
            band = jnp.where(mine, jnp.where(ids - b * nb == rid, 1.0, 0.0), band)
            done = dot_f32(small, band, ((1,), (0,)), mode)
            kept = jnp.where(ids < (b + 1) * nb, done, 0.0)
            for h in range(halves):
                system[h, here, :] = kept[:, h * 128 : (h + 1) * 128]
            rest = members - (b + 1) * nb
            if rest:
                below = pl.ds(pl.multiple_of(start + nb, nb), rest)
                change = dot_f32(done[:, (b + 1) * nb :], done, ((0,), (0,)), mode)
                for h in range(halves):
                    old = system[h, below, :]
                    if h == half:
                        hl = lax.broadcasted_iota(jnp.int32, (rest, 128), 1)
                        old = jnp.where((hl >= place) & (hl < place + nb), 0.0, old)
                    system[h, below, :] = old - change[:, h * 128 : (h + 1) * 128]
            return carry

        lax.fori_loop(0, regions, sweep, 0)

    def finish(r, carry):
        at = pl.ds(pl.multiple_of(r * members, members), members)
        inverse = jnp.concatenate([system[h, at, :] for h in range(halves)], axis=1)
        shares = shares_of(r)
        root = jnp.sqrt(members * shares)
        solved = jnp.sum(inverse * inv[pl.ds(r, 1), :], axis=1, keepdims=True)
        weights = jnp.sum(inverse * solved, axis=0, keepdims=True)
        mixing = root * (weights + math.sqrt(members - 1.0) * inverse)
        mixing = mixing - jnp.sum(mixing, axis=1, keepdims=True) * shares + shares
        high, low = split(mixing)
        states = state_ref[:, r].reshape(members, state_ref.shape[3])
        done = dot(high, states, ((1,), (0,))) + dot(low, states, ((1,), (0,)))
        out_ref[:, r] = done.astype(BF16).reshape(mems, members_dev, state_ref.shape[3])
        return carry

    lax.fori_loop(0, regions, finish, 0)


def analysis_scratch(members, regions, slots, width, nb):
    return [
        pltpu.VMEM((members, slots * width), BF16),
        pltpu.VMEM((16, slots * width), F32),
        pltpu.VMEM((members // 128, regions * members, 128), F32),
        pltpu.VMEM((regions * nb, 128), F32),
        pltpu.VMEM((regions, members), F32),
        pltpu.VMEM((regions, members, 128), F32),
    ]


def collect(list_ref, all_ref, out_ref):
    rows, slots = list_ref.shape

    def one(r, carry):
        for l in range(slots):
            out_ref[r * slots + l] = all_ref[list_ref[r, l]]
        return carry

    lax.fori_loop(0, rows, one, 0)


def analyse_here(*refs, nb, group, mode):
    analyse(lax.axis_index("mem"), *refs, nb=nb, group=group, mode=mode)


SMEM = pl.BlockSpec(memory_space=pltpu.SMEM)
VMEM = pl.BlockSpec(memory_space=pltpu.VMEM)


def body(
    ensemble_state, obs_ens, innovation, obs_prec, block_list, block_count, loc_weight, prior_weight
):
    mems = lax.axis_size("mem")
    members_dev, regions_dev, p_size = ensemble_state.shape
    width = obs_ens.shape[2]
    slots = block_list.shape[1]
    regions = regions_dev // mems
    entries = regions * slots
    members = members_dev * mems
    params = pltpu.CompilerParams(vmem_limit_bytes=56 << 20)

    table = jnp.concatenate([obs_prec, innovation], axis=1)
    table = lax.all_gather(table, "space", axis=0, tiled=True)
    blocks = jnp.transpose(obs_ens, (1, 0, 2))
    blocks = lax.all_gather(blocks, "space", axis=0, tiled=True)
    states = jnp.transpose(ensemble_state, (1, 0, 2))
    states = lax.all_to_all(states, "mem", split_axis=0, concat_axis=0, tiled=True)
    states = states.reshape(mems, regions, members_dev, p_size)
    listed = pl.pallas_call(
        collect,
        in_specs=[SMEM, VMEM],
        out_specs=VMEM,
        out_shape=jax.ShapeDtypeStruct((regions_dev * slots, members_dev, width), BF16),
        compiler_params=params,
    )(block_list, blocks)
    seen = lax.all_to_all(listed, "mem", split_axis=0, concat_axis=0, tiled=True)
    seen = seen.reshape(mems, entries, members_dev, width)
    nb = 64
    updated = pl.pallas_call(
        functools.partial(analyse_here, nb=nb, group=8, mode=6),
        in_specs=[SMEM, SMEM, SMEM, VMEM, VMEM, VMEM, VMEM],
        out_specs=VMEM,
        out_shape=jax.ShapeDtypeStruct((mems, regions, members_dev, p_size), BF16),
        scratch_shapes=analysis_scratch(members, regions, slots, width, nb),
        compiler_params=params,
    )(block_list, block_count, loc_weight, table, prior_weight, seen, states)
    updated = updated.reshape(regions_dev, members_dev, p_size)
    updated = lax.all_to_all(updated, "mem", split_axis=0, concat_axis=0, tiled=True)
    return jnp.transpose(updated, (1, 0, 2))


def solution(mesh):
    return jax.shard_map(
        body,
        mesh=mesh,
        in_specs=(
            P("mem", "space", None),
            P("mem", "space", None),
            P("space", None),
            P("space", None),
            P("space", None),
            P("space"),
            P("space", None),
            P("space", None),
        ),
        out_specs=P("mem", "space", None),
        check_vma=False,
    )
```

```python
import functools
import math

import jax
import jax.numpy as jnp
from jax import lax
from jax.experimental import pallas as pl
from jax.experimental.pallas import tpu as pltpu
from jax.sharding import PartitionSpec as P

INFLATION = 1.1
HIGHEST = lax.Precision.HIGHEST
F32 = jnp.float32
BF16 = jnp.bfloat16


def dot(a, b, dims, precision=None):
    return lax.dot_general(a, b, (dims, ((), ())), precision=precision, preferred_element_type=F32)


def split(x):
    high = x.astype(BF16)
    return high, (x - high.astype(F32)).astype(BF16)


def dot_f32(a, b, dims, mode):
    if mode == 6:
        return dot(a, b, dims, HIGHEST)
    ah, al = split(a)
    bh, bl = split(b)
    return dot(ah, bh, dims) + (dot(ah, bl, dims) + dot(al, bh, dims))


def eliminate(rows, group):
    count = len(rows)
    rows = list(rows)

    def lane(x, i):
        return jnp.broadcast_to(x[:, i : i + 1], x.shape)

    for k in range(0, count, group):
        small = {(a, b): lane(rows[k + a], k + b) for a in range(group) for b in range(a, group)}
        for a in range(group):
            root = lax.rsqrt(small[a, a])
            upper = {b: small[a, b] * root for b in range(a + 1, group)}
            rows[k + a] = rows[k + a] * root
            for c in range(a + 1, group):
                rows[k + c] = rows[k + c] - upper[c] * rows[k + a]
                for b in range(c, group):
                    small[c, b] = small[c, b] - upper[c] * upper[b]
        for i in range(k + group, count):
            for a in range(group):
                rows[i] = rows[i] - lane(rows[k + a], i) * rows[k + a]
    return rows


def analyse(
    me, list_ref, count_ref, loc_ref, table_ref, prior_ref, obs_ref, state_ref, out_ref,
    seen, extra, system, diag, inv, qcol, *, nb, group, mode,
):
    pieces, mems, entries, part, width = obs_ref.shape
    members_dev = pieces * part
    members = mems * members_dev
    slots = list_ref.shape[1]
    regions = entries // slots
    first = me * regions
    shares_all = prior_ref[pl.ds(first, regions), :]
    shares_all = shares_all / jnp.sum(shares_all, axis=1, keepdims=True)
    root_all = jnp.sqrt(members * shares_all)
    root_t = jnp.transpose(root_all)
    for r in range(regions):
        qcol[r] = jnp.broadcast_to(root_t[:, r : r + 1], (members, 128))
    extra[...] = jnp.zeros_like(extra)
    row_id = lax.broadcasted_iota(jnp.int32, (members, members), 0)
    col_id = lax.broadcasted_iota(jnp.int32, (members, members), 1)
    vec_scr = []

    def shares_of(r):
        s = prior_ref[pl.ds(first + r, 1), :]
        return s / jnp.sum(s, axis=1, keepdims=True)

    def build(r, carry):
        row = first + r
        for l in range(slots):
            block = list_ref[row, l]
            both = table_ref[pl.ds(block, 1), :]
            live = jnp.where(l < count_ref[row], loc_ref[row, l], 0.0)
            scale = jnp.sqrt(live * both[:, :width])
            picked = jnp.concatenate(
                [obs_ref[p, m, r * slots + l] for m in range(mems) for p in range(pieces)], axis=0
            ).astype(F32)
            cols = slice(l * width, (l + 1) * width)
            seen[:, cols] = (picked * scale).astype(BF16)
            high, low = split(scale * both[:, width:])
            extra[0:1, cols] = high.astype(F32)
            extra[1:2, cols] = low.astype(F32)
        all_seen = seen[...]
        gram = dot(all_seen, all_seen, ((1,), (1,)))
        proj = dot(extra[...].astype(BF16), all_seen, ((1,), (1,)))
        proj = proj[0:1] + proj[1:2]
        shares = shares_of(r)
        root = jnp.sqrt(members * shares)
        left = dot(jnp.broadcast_to(shares, (8, members)), gram, ((1,), (0,)), HIGHEST)[0:1]
        centred = gram - left
        centred = centred - jnp.sum(centred * shares, axis=1, keepdims=True)
        q = jnp.concatenate([qcol[r]] * (members // 128), axis=1)
        full = q * centred * root + jnp.where(row_id == col_id, (members - 1) / INFLATION, 0.0)
        at = pl.ds(pl.multiple_of(r * members, members), members)
        for half in range(members // 128):
            system[half, at, :] = full[:, half * 128 : (half + 1) * 128]
        vector = root * (proj - jnp.sum(shares * proj, axis=1, keepdims=True))
        inv[pl.ds(r, 1), :] = vector
        return carry

    lax.fori_loop(0, regions, build, 0)

    lane_id = lax.broadcasted_iota(jnp.int32, (regions, 128), 1)
    halves = members // 128
    per_half = 128 // nb
    for b in range(members // nb):
        half, place = b // per_half, (b % per_half) * nb
        def factor(_, carry):
            rows = []
            for i in range(nb):
                x = system[half, pl.ds(b * nb + i, regions, stride=members), :]
                if place:
                    x = pltpu.roll(x, 128 - place, 1)
                rows.append(jnp.where(lane_id < nb, x, jnp.where(lane_id == nb + i, 1.0, 0.0)))
            rows = eliminate(rows, group)
            for i in range(nb):
                diag[pl.ds(i, regions, stride=nb), :] = rows[i]
            return carry

        factor(0, 0)

        def sweep(r, carry):
            start = r * members + b * nb
            here = pl.ds(pl.multiple_of(start, nb), nb)
            small = diag[pl.ds(pl.multiple_of(r * nb, nb), nb), :][:, nb : 2 * nb]
            band = jnp.concatenate([system[h, here, :] for h in range(halves)], axis=1)
            ids = lax.broadcasted_iota(jnp.int32, (nb, members), 1)
            rid = lax.broadcasted_iota(jnp.int32, (nb, members), 0)
            mine = (ids >= b * nb) & (ids < (b + 1) * nb)
            band = jnp.where(mine, jnp.where(ids - b * nb == rid, 1.0, 0.0), band)
            done = dot_f32(small, band, ((1,), (0,)), mode)
            kept = jnp.where(ids < (b + 1) * nb, done, 0.0)
            for h in range(halves):
                system[h, here, :] = kept[:, h * 128 : (h + 1) * 128]
            rest = members - (b + 1) * nb
            if rest:
                below = pl.ds(pl.multiple_of(start + nb, nb), rest)
                change = dot_f32(done[:, (b + 1) * nb :], done, ((0,), (0,)), mode)
                for h in range(halves):
                    old = system[h, below, :]
                    if h == half:
                        hl = lax.broadcasted_iota(jnp.int32, (rest, 128), 1)
                        old = jnp.where((hl >= place) & (hl < place + nb), 0.0, old)
                    system[h, below, :] = old - change[:, h * 128 : (h + 1) * 128]
            return carry

        lax.fori_loop(0, regions, sweep, 0)

    def finish(r, carry):
        at = pl.ds(pl.multiple_of(r * members, members), members)
        inverse = jnp.concatenate([system[h, at, :] for h in range(halves)], axis=1)
        shares = shares_of(r)
        root = jnp.sqrt(members * shares)
        solved = jnp.sum(inverse * inv[pl.ds(r, 1), :], axis=1, keepdims=True)
        weights = jnp.sum(inverse * solved, axis=0, keepdims=True)
        mixing = root * (weights + math.sqrt(members - 1.0) * inverse)
        mixing = mixing - jnp.sum(mixing, axis=1, keepdims=True) * shares + shares
        high, low = split(mixing)
        states = state_ref[:, r].reshape(members, state_ref.shape[3])
        done = dot(high, states, ((1,), (0,))) + dot(low, states, ((1,), (0,)))
        out_ref[:, r] = done.astype(BF16).reshape(mems, members_dev, state_ref.shape[3])
        return carry

    lax.fori_loop(0, regions, finish, 0)


def analysis_scratch(members, regions, slots, width, nb):
    return [
        pltpu.VMEM((members, slots * width), BF16),
        pltpu.VMEM((16, slots * width), F32),
        pltpu.VMEM((members // 128, regions * members, 128), F32),
        pltpu.VMEM((regions * nb, 128), F32),
        pltpu.VMEM((regions, members), F32),
        pltpu.VMEM((regions, members, 128), F32),
    ]


def exchange(
    list_ref, own_ref, obs_ref, listed, send_sem, recv_sem, out_sem, in_sem, own_sem, *blocks, side
):
    pieces, count = own_ref.shape[:2]
    mems, entries = obs_ref.shape[1:3]
    slots = list_ref.shape[1]
    half = count // 2
    space, mem = lax.axis_index("space"), lax.axis_index("mem")
    x, z = space // side, space % side

    def at(axis, i, j):
        dx, dz = (i, j) if axis == 0 else (j, i)
        return (x + dx + side) % side * side + (z + dz + side) % side

    barrier = pltpu.get_barrier_semaphore()
    near = [at(0, 1, 0), at(0, -1, 0), at(0, 0, 1), at(0, 0, -1)]
    for there in near:
        pl.semaphore_signal(barrier, inc=1, device_id={"space": there, "mem": mem})
    for step in range(1, mems):
        pl.semaphore_signal(barrier, inc=1, device_id={"space": space, "mem": (mem + step) % mems})

    own_copies = [
        pltpu.make_async_copy(
            own_ref.at[p], blocks[p].at[pl.ds(pl.multiple_of(space * count, count), count)], own_sem.at[p]
        )
        for p in range(pieces)
    ]
    for copy in own_copies:
        copy.start()
    pl.semaphore_wait(barrier, 4 + mems - 1)

    def send(p, axis, number, chunk, part, to, own=False):
        start, size = {"all": (0, half), "low": (0, half // 2), "high": (half // 2, half // 2)}[part]
        start = start + axis * half
        rows = pl.ds(pl.multiple_of(chunk * count + start, size), size)
        src = own_ref.at[p, pl.ds(start, size)] if own else blocks[p].at[rows]
        return pltpu.make_async_remote_copy(
            src_ref=src,
            dst_ref=blocks[p].at[rows],
            send_sem=send_sem.at[p, axis, number],
            recv_sem=recv_sem.at[p, axis, number],
            device_id={"space": to, "mem": mem},
        )

    order = (0, -1, 1, 2)
    sent = []

    def copy_of(p, axis, number):
        if number == 0:
            return send(p, axis, 0, at(axis, 0, 0), "all", at(axis, 1, 0), True)
        if number == 1:
            return send(p, axis, 1, at(axis, 0, 0), "all", at(axis, -1, 0), True)
        if number == 2:
            return send(p, axis, 2, at(axis, -1, 0), "low", at(axis, 1, 0))
        if number == 3:
            return send(p, axis, 3, at(axis, 1, 0), "high", at(axis, -1, 0))
        j, kind = (number - 4) // 4, (number - 4) % 4
        d = order[j]
        if kind == 0:
            return send(p, axis, number, at(axis, d, 0), "all", at(axis, 0, 1), d == 0)
        if kind == 1:
            return send(p, axis, number, at(axis, d, 0), "all", at(axis, 0, -1), d == 0)
        if kind == 2:
            return send(p, axis, number, at(axis, d, -1), "low", at(axis, 0, 1))
        return send(p, axis, number, at(axis, d, 1), "high", at(axis, 0, -1))

    def start(p, *numbers):
        for number in numbers:
            for axis in (0, 1):
                copy = copy_of(p, axis, number)
                copy.start()
                sent.append(copy)

    def arrive(p, axis, *numbers):
        for number in numbers:
            copy_of(p, axis, number).wait_recv()

    def begin(p):
        start(p, 0, 1, 4, 5)

    outgoing = []
    begin(0)
    for p in range(pieces):
        for axis in (0, 1):
            arrive(p, axis, 0)
        start(p, 2, 8, 9)
        for axis in (0, 1):
            arrive(p, axis, 1)
        start(p, 3, 12, 13)
        for axis in (0, 1):
            arrive(p, axis, 2, 3)
        start(p, 16, 17)
        if p + 1 < pieces:
            begin(p + 1)
        for j in range(4):
            for kind in (0, 1):
                for axis in (0, 1):
                    arrive(p, axis, 4 + 4 * j + kind)
                start(p, 4 + 4 * j + kind + 2)
        for j in range(4):
            for axis in (0, 1):
                arrive(p, axis, 6 + 4 * j, 7 + 4 * j)
        own_copies[p].wait()

        def pick(r, carry, p=p):
            for l in range(slots):
                listed[p, r * slots + l] = blocks[p][list_ref[r, l]]
            return carry

        lax.fori_loop(0, list_ref.shape[0], pick, 0)
        mine = pltpu.make_async_copy(
            listed.at[p, pl.ds(pl.multiple_of(mem * entries, entries), entries)],
            obs_ref.at[p, mem],
            own_sem.at[pieces + p],
        )
        mine.start()
        own_copies.append(mine)
        for step in range(1, mems):
            to = (mem + step) % mems
            copy = pltpu.make_async_remote_copy(
                src_ref=listed.at[p, pl.ds(pl.multiple_of(to * entries, entries), entries)],
                dst_ref=obs_ref.at[p, mem],
                send_sem=out_sem.at[p, step],
                recv_sem=in_sem.at[p, step],
                device_id={"space": space, "mem": to},
            )
            copy.start()
            outgoing.append((p, step, copy))

    for p in range(pieces):
        own_copies[pieces + p].wait()
    for p, step, copy in outgoing:
        source = (mem - step + mems) % mems
        pltpu.make_async_remote_copy(
            src_ref=listed.at[p, pl.ds(0, entries)],
            dst_ref=obs_ref.at[p, source],
            send_sem=out_sem.at[p, step],
            recv_sem=in_sem.at[p, step],
            device_id={"space": space, "mem": source},
        ).wait_recv()
        copy.wait_send()
    for copy in sent:
        copy.wait_send()


def analyse_here(*refs, nb, group, mode):
    analyse(lax.axis_index("mem"), *refs, nb=nb, group=group, mode=mode)


SMEM = pl.BlockSpec(memory_space=pltpu.SMEM)
VMEM = pl.BlockSpec(memory_space=pltpu.VMEM)


def body(
    ensemble_state, obs_ens, innovation, obs_prec, block_list, block_count, loc_weight, prior_weight
):
    spaces, mems = lax.axis_size("space"), lax.axis_size("mem")
    members_dev, regions_dev, p_size = ensemble_state.shape
    blocks_dev, width = obs_ens.shape[1:]
    slots = block_list.shape[1]
    regions = regions_dev // mems
    entries = regions * slots
    members = members_dev * mems
    pieces = 2
    part = members_dev // pieces
    dma = pltpu.SemaphoreType.DMA

    table = jnp.concatenate([obs_prec, innovation], axis=1)
    table = lax.all_gather(table, "space", axis=0, tiled=True)
    states = jnp.transpose(ensemble_state, (1, 0, 2))
    states = lax.all_to_all(states, "mem", split_axis=0, concat_axis=0, tiled=True)
    states = states.reshape(mems, regions, members_dev, p_size)
    own = jnp.transpose(obs_ens.reshape(pieces, part, blocks_dev, width), (0, 2, 1, 3))
    seen = pl.pallas_call(
        functools.partial(exchange, side=math.isqrt(spaces)),
        in_specs=[SMEM, VMEM],
        out_specs=VMEM,
        out_shape=jax.ShapeDtypeStruct((pieces, mems, entries, part, width), BF16),
        scratch_shapes=[
            pltpu.VMEM((pieces, regions_dev * slots, part, width), BF16),
            dma((pieces, 2, 20)),
            dma((pieces, 2, 20)),
            dma((pieces, mems)),
            dma((pieces, mems)),
            dma((2 * pieces,)),
            *[pltpu.VMEM((blocks_dev * spaces, part, width), BF16) for _ in range(pieces)],
        ],
        compiler_params=pltpu.CompilerParams(
            vmem_limit_bytes=48 << 20, collective_id=0, has_side_effects=True
        ),
    )(block_list, own)
    nb = 64
    updated = pl.pallas_call(
        functools.partial(analyse_here, nb=nb, group=8, mode=6),
        in_specs=[SMEM, SMEM, SMEM, VMEM, VMEM, VMEM, VMEM],
        out_specs=VMEM,
        out_shape=jax.ShapeDtypeStruct((mems, regions, members_dev, p_size), BF16),
        scratch_shapes=analysis_scratch(members, regions, slots, width, nb),
        compiler_params=pltpu.CompilerParams(vmem_limit_bytes=48 << 20),
    )(block_list, block_count, loc_weight, table, prior_weight, seen, states)
    updated = updated.reshape(regions_dev, members_dev, p_size)
    updated = lax.all_to_all(updated, "mem", split_axis=0, concat_axis=0, tiled=True)
    return jnp.transpose(updated, (1, 0, 2))


def solution(mesh):
    return jax.shard_map(
        body,
        mesh=mesh,
        in_specs=(
            P("mem", "space", None),
            P("mem", "space", None),
            P("space", None),
            P("space", None),
            P("space", None),
            P("space"),
            P("space", None),
            P("space", None),
        ),
        out_specs=P("mem", "space", None),
        check_vma=False,
    )
```

```python
import functools
import math

import jax
import jax.numpy as jnp
from jax import lax
from jax.experimental import pallas as pl
from jax.experimental.pallas import tpu as pltpu
from jax.sharding import PartitionSpec as P

INFLATION = 1.1
HIGHEST = lax.Precision.HIGHEST
F32 = jnp.float32
BF16 = jnp.bfloat16


def dot(a, b, dims, precision=None):
    return lax.dot_general(a, b, (dims, ((), ())), precision=precision, preferred_element_type=F32)


def split(x):
    high = x.astype(BF16)
    return high, (x - high.astype(F32)).astype(BF16)


def eliminate(rows, group):
    count = len(rows)
    rows = list(rows)

    def lane(x, i):
        return jnp.broadcast_to(x[:, i : i + 1], x.shape)

    for k in range(0, count, group):
        small = {(a, b): lane(rows[k + a], k + b) for a in range(group) for b in range(a, group)}
        for a in range(group):
            root = lax.rsqrt(small[a, a])
            upper = {b: small[a, b] * root for b in range(a + 1, group)}
            rows[k + a] = rows[k + a] * root
            for c in range(a + 1, group):
                rows[k + c] = rows[k + c] - upper[c] * rows[k + a]
                for b in range(c, group):
                    small[c, b] = small[c, b] - upper[c] * upper[b]
        for i in range(k + group, count):
            for a in range(group):
                rows[i] = rows[i] - lane(rows[k + a], i) * rows[k + a]
    return rows


def whole(
    list_ref, count_ref, loc_ref, state_ref, obs_ref, prec_ref, innov_ref, prior_ref,
    out_ref,
    listed, seen_obs, table, states_in, wide, result, seen, extra, system, diag, vectors, qcol,
    ring_send, ring_recv, obs_send, obs_recv, state_send, state_recv, out_send, out_recv, own_sem,
    table_send, table_recv,
    *blocks, side, nb, group,
):
    pieces, mems, entries, part, width = seen_obs.shape
    members_dev, count = obs_ref.shape[:2]
    rows_space, slots = list_ref.shape
    regions = rows_space // mems
    members = mems * members_dev
    p_size = state_ref.shape[2]
    half = count // 2
    space, mem = lax.axis_index("space"), lax.axis_index("mem")
    core = mem % 2
    x, z = space // side, space % side
    first = mem * regions

    def at(axis, i, j):
        dx, dz = (i, j) if axis == 0 else (j, i)
        return (x + dx + side) % side * side + (z + dz + side) % side

    def peer(step):
        return (mem + step) % mems

    barrier = pltpu.get_barrier_semaphore()
    for there in [at(0, 1, 0), at(0, -1, 0), at(0, 0, 1), at(0, 0, -1)]:
        pl.semaphore_signal(barrier, inc=1, device_id={"space": there, "mem": mem})
    for step in range(1, mems):
        pl.semaphore_signal(barrier, inc=1, device_id={"space": space, "mem": peer(step)})

    for k in range(members_dev):
        wide[0, k * count : (k + 1) * count, :] = obs_ref[k].astype(F32)

    def turn(b, carry):
        block = wide[0, pl.ds(b, members_dev, stride=count), :].astype(BF16)
        for p in range(pieces):
            blocks[p][space * count + b] = block[p * part : (p + 1) * part]
        return carry

    lax.fori_loop(0, count, turn, 0, unroll=4)
    here = pl.ds(pl.multiple_of(space * count, count), count)
    table[core, here, :] = jnp.where(core == 0, prec_ref[...], innov_ref[...])
    pl.semaphore_wait(barrier, 4 + mems - 1)

    rings = [*blocks, table.at[core]]

    def send(p, axis, number, chunk, share, to):
        start, size = {"all": (0, half), "low": (0, half // 2), "high": (half // 2, half // 2)}[share]
        rows = pl.ds(pl.multiple_of(chunk * count + start + axis * half, size), size)
        return pltpu.make_async_remote_copy(
            src_ref=rings[p].at[rows],
            dst_ref=rings[p].at[rows],
            send_sem=ring_send.at[p, axis, number],
            recv_sem=ring_recv.at[p, axis, number],
            device_id={"space": to, "mem": mem},
        )

    order = (0, -1, 1, 2)

    def copy_of(p, axis, number):
        if number == 0:
            return send(p, axis, 0, at(axis, 0, 0), "all", at(axis, 1, 0))
        if number == 1:
            return send(p, axis, 1, at(axis, 0, 0), "all", at(axis, -1, 0))
        if number == 2:
            return send(p, axis, 2, at(axis, -1, 0), "low", at(axis, 1, 0))
        if number == 3:
            return send(p, axis, 3, at(axis, 1, 0), "high", at(axis, -1, 0))
        d, kind = order[(number - 4) // 4], (number - 4) % 4
        if kind == 0:
            return send(p, axis, number, at(axis, d, 0), "all", at(axis, 0, 1))
        if kind == 1:
            return send(p, axis, number, at(axis, d, 0), "all", at(axis, 0, -1))
        if kind == 2:
            return send(p, axis, number, at(axis, d, -1), "low", at(axis, 0, 1))
        return send(p, axis, number, at(axis, d, 1), "high", at(axis, 0, -1))

    sent = []

    def start(p, *numbers):
        for number in numbers:
            for axis in (0, 1):
                copy = copy_of(p, axis, number)
                copy.start()
                sent.append(copy)

    def arrive(p, *numbers):
        for number in numbers:
            for axis in (0, 1):
                copy_of(p, axis, number).wait_recv()

    def begin(p):
        start(p, 0, 1, 4, 5)

    def state_copy(step):
        to = peer(step)
        return pltpu.make_async_remote_copy(
            src_ref=state_ref.at[:, pl.ds(pl.multiple_of(to * regions, regions), regions), :],
            dst_ref=states_in.at[mem],
            send_sem=state_send.at[step],
            recv_sem=state_recv.at[step],
            device_id={"space": space, "mem": to},
        )

    def obs_copy(p, step):
        to = peer(step)
        return pltpu.make_async_remote_copy(
            src_ref=listed.at[p, pl.ds(pl.multiple_of(to * entries, entries), entries)],
            dst_ref=seen_obs.at[p, mem],
            send_sem=obs_send.at[p, step],
            recv_sem=obs_recv.at[p, step],
            device_id={"space": space, "mem": to},
        )

    local = []

    def begin_states():
        copy = pltpu.make_async_copy(
            state_ref.at[:, pl.ds(pl.multiple_of(first, regions), regions), :],
            states_in.at[mem],
            own_sem.at[pieces],
        )
        copy.start()
        local.append(copy)
        for step in range(1, mems):
            state_copy(step).start()

    sequence = [0, pieces, *range(1, pieces)]
    begin(0)
    begin_states()
    for turn_number, p in enumerate(sequence):
        arrive(p, 0)
        start(p, 2, 8, 9)
        arrive(p, 1)
        start(p, 3, 12, 13)
        arrive(p, 2, 3)
        start(p, 16, 17)
        if turn_number + 1 < len(sequence):
            begin(sequence[turn_number + 1])
        for j in range(4):
            for kind in (0, 1):
                arrive(p, 4 + 4 * j + kind)
                start(p, 4 + 4 * j + kind + 2)
        for j in range(4):
            arrive(p, 6 + 4 * j, 7 + 4 * j)
        if p == pieces:
            other = pltpu.make_async_remote_copy(
                src_ref=table.at[core],
                dst_ref=table.at[core],
                send_sem=table_send,
                recv_sem=table_recv,
                device_id={"space": space, "mem": mem + 1 - 2 * core},
            )
            other.start()
            continue

        def pick(r, carry, p=p):
            for l in range(slots):
                listed[p, r * slots + l] = blocks[p][list_ref[r, l]]
            return carry

        lax.fori_loop(0, rows_space, pick, 0)
        mine = pltpu.make_async_copy(
            listed.at[p, pl.ds(pl.multiple_of(mem * entries, entries), entries)],
            seen_obs.at[p, mem],
            own_sem.at[p],
        )
        mine.start()
        local.append(mine)
        for step in range(1, mems):
            obs_copy(p, step).start()

    extra[...] = jnp.zeros_like(extra)
    shares_all = prior_ref[pl.ds(pl.multiple_of(first, regions), regions), :]
    shares_all = shares_all / jnp.sum(shares_all, axis=1, keepdims=True)
    root_t = jnp.transpose(jnp.sqrt(members * shares_all))
    for r in range(regions):
        qcol[r] = jnp.broadcast_to(root_t[:, r : r + 1], (members, 128))
    halves = members // 128
    for step in range(1, mems):
        state_copy(step).wait_recv()
    local[0].wait()
    for m in range(mems):
        many = states_in[m].astype(F32).reshape(members_dev * regions, p_size)
        for h in range(p_size // 128):
            wide[h, m * members_dev * regions : (m + 1) * members_dev * regions, :] = many[
                :, h * 128 : (h + 1) * 128
            ]
    other.wait()
    for copy in sent:
        copy.wait_send()
    for step in range(1, mems):
        state_copy(step).wait_send()
    for copy in local[1:]:
        copy.wait()
    for p in range(pieces):
        for step in range(1, mems):
            obs_copy(p, step).wait()

    row_id = lax.broadcasted_iota(jnp.int32, (members, members), 0)
    col_id = lax.broadcasted_iota(jnp.int32, (members, members), 1)

    def shares_of(r):
        s = prior_ref[pl.ds(first + r, 1), :]
        return s / jnp.sum(s, axis=1, keepdims=True)

    def build(r, carry):
        row = first + r
        for l in range(slots):
            block = list_ref[row, l]
            live = jnp.where(l < count_ref[row], loc_ref[row, l], 0.0)
            scale = jnp.sqrt(live * table[0, pl.ds(block, 1), :])
            picked = jnp.concatenate(
                [seen_obs[p, m, r * slots + l] for m in range(mems) for p in range(pieces)], axis=0
            ).astype(F32)
            cols = slice(l * width, (l + 1) * width)
            seen[:, cols] = (picked * scale).astype(BF16)
            high, low = split(scale * table[1, pl.ds(block, 1), :])
            extra[0:1, cols] = high.astype(F32)
            extra[1:2, cols] = low.astype(F32)
        all_seen = seen[...]
        gram = dot(all_seen, all_seen, ((1,), (1,)))
        proj = dot(extra[...].astype(BF16), all_seen, ((1,), (1,)))
        proj = proj[0:1] + proj[1:2]
        shares = shares_of(r)
        root = jnp.sqrt(members * shares)
        left = dot(jnp.broadcast_to(shares, (8, members)), gram, ((1,), (0,)), HIGHEST)[0:1]
        centred = gram - left
        centred = centred - jnp.sum(centred * shares, axis=1, keepdims=True)
        q = jnp.concatenate([qcol[r]] * halves, axis=1)
        full = q * centred * root + jnp.where(row_id == col_id, (members - 1) / INFLATION, 0.0)
        at_r = pl.ds(pl.multiple_of(r * members, members), members)
        for h in range(halves):
            system[h, at_r, :] = full[:, h * 128 : (h + 1) * 128]
        vectors[pl.ds(r, 1), :] = root * (proj - jnp.sum(shares * proj, axis=1, keepdims=True))
        return carry

    lax.fori_loop(0, regions, build, 0, unroll=2)

    lane_id = lax.broadcasted_iota(jnp.int32, (regions, 128), 1)
    for b in range(members // nb):
        h_b, place = b * nb // 128, b * nb % 128
        rows = []
        for i in range(nb):
            row = system[h_b, pl.ds(b * nb + i, regions, stride=members), :]
            if place:
                row = pltpu.roll(row, 128 - place, 1)
            rows.append(jnp.where(lane_id < nb, row, jnp.where(lane_id == nb + i, 1.0, 0.0)))
        rows = eliminate(rows, group)
        for i in range(nb):
            diag[pl.ds(i, regions, stride=nb), :] = rows[i]

        def sweep(r, carry, b=b, h_b=h_b, place=place):
            begins = r * members + b * nb
            band_rows = pl.ds(pl.multiple_of(begins, nb), nb)
            small = diag[pl.ds(pl.multiple_of(r * nb, nb), nb), :][:, nb : 2 * nb]
            band = jnp.concatenate([system[h, band_rows, :] for h in range(halves)], axis=1)
            ids = lax.broadcasted_iota(jnp.int32, (nb, members), 1)
            rid = lax.broadcasted_iota(jnp.int32, (nb, members), 0)
            mine = (ids >= b * nb) & (ids < (b + 1) * nb)
            band = jnp.where(mine, jnp.where(ids - b * nb == rid, 1.0, 0.0), band)
            done = dot(small, band, ((1,), (0,)), HIGHEST)
            kept = jnp.where(ids < (b + 1) * nb, done, 0.0)
            for h in range(halves):
                system[h, band_rows, :] = kept[:, h * 128 : (h + 1) * 128]
            rest = members - (b + 1) * nb
            if rest:
                below = pl.ds(pl.multiple_of(begins + nb, nb), rest)
                change = dot(done[:, (b + 1) * nb :], done, ((0,), (0,)), HIGHEST)
                for h in range(halves):
                    old = system[h, below, :]
                    if h == h_b:
                        lanes = lax.broadcasted_iota(jnp.int32, (rest, 128), 1)
                        old = jnp.where((lanes >= place) & (lanes < place + nb), 0.0, old)
                    system[h, below, :] = old - change[:, h * 128 : (h + 1) * 128]
            return carry

        lax.fori_loop(0, regions, sweep, 0, unroll=True)

    def out_copy(r, step):
        to = peer(step)
        return pltpu.make_async_remote_copy(
            src_ref=result.at[r, pl.ds(pl.multiple_of(to * members_dev, members_dev), members_dev), :],
            dst_ref=out_ref.at[first + r],
            send_sem=out_send.at[r, step],
            recv_sem=out_recv.at[r, step],
            device_id={"space": space, "mem": to},
        )

    def own_out(r):
        return pltpu.make_async_copy(
            result.at[r, pl.ds(pl.multiple_of(mem * members_dev, members_dev), members_dev), :],
            out_ref.at[first + r],
            out_send.at[r, 0],
        )

    def finish(r, carry):
        at_r = pl.ds(pl.multiple_of(r * members, members), members)
        inverse = jnp.concatenate([system[h, at_r, :] for h in range(halves)], axis=1)
        shares = shares_of(r)
        root = jnp.sqrt(members * shares)
        solved = jnp.sum(inverse * vectors[pl.ds(r, 1), :], axis=1, keepdims=True)
        weights = jnp.sum(inverse * solved, axis=0, keepdims=True)
        mixing = root * (weights + math.sqrt(members - 1.0) * inverse)
        mixing = mixing - jnp.sum(mixing, axis=1, keepdims=True) * shares + shares
        high, low = split(mixing)
        states = jnp.concatenate(
            [wide[h, pl.ds(r, members, stride=regions), :] for h in range(p_size // 128)], axis=1
        ).astype(BF16)
        done = dot(high, states, ((1,), (0,))) + dot(low, states, ((1,), (0,)))
        result[r] = done.astype(BF16)
        own_out(r).start()
        for step in range(1, mems):
            out_copy(r, step).start()
        return carry

    lax.fori_loop(0, regions, finish, 0)

    def close(r, carry):
        own_out(r).wait()
        for step in range(1, mems):
            out_copy(r, step).wait()
        return carry

    lax.fori_loop(0, regions, close, 0)


SMEM = pl.BlockSpec(memory_space=pltpu.SMEM)
VMEM = pl.BlockSpec(memory_space=pltpu.VMEM)
ANY = pl.BlockSpec(memory_space=pl.ANY)


def body(
    ensemble_state, obs_ens, innovation, obs_prec, block_list, block_count, loc_weight, prior_weight
):
    spaces, mems = lax.axis_size("space"), lax.axis_size("mem")
    members_dev, regions_dev, p_size = ensemble_state.shape
    blocks_dev, width = obs_ens.shape[1:]
    slots = block_list.shape[1]
    regions = regions_dev // mems
    entries = regions * slots
    members = members_dev * mems
    pieces = 4
    part = members_dev // pieces
    nb = 64
    dma = pltpu.SemaphoreType.DMA
    updated = pl.pallas_call(
        functools.partial(whole, side=math.isqrt(spaces), nb=nb, group=8),
        in_specs=[SMEM, SMEM, SMEM, ANY, VMEM, VMEM, VMEM, VMEM],
        out_specs=VMEM,
        out_shape=jax.ShapeDtypeStruct((regions_dev, members_dev, p_size), BF16),
        scratch_shapes=[
            pltpu.VMEM((pieces, regions_dev * slots, part, width), BF16),
            pltpu.VMEM((pieces, mems, entries, part, width), BF16),
            pltpu.VMEM((2, blocks_dev * spaces, width), F32),
            pltpu.VMEM((mems, members_dev, regions, p_size), BF16),
            pltpu.VMEM((p_size // 128, max(members * regions, members_dev * blocks_dev), 128), F32),
            pltpu.VMEM((regions, members, p_size), BF16),
            pltpu.VMEM((members, slots * width), BF16),
            pltpu.VMEM((16, slots * width), F32),
            pltpu.VMEM((members // 128, regions * members, 128), F32),
            pltpu.VMEM((regions * nb, 128), F32),
            pltpu.VMEM((regions, members), F32),
            pltpu.VMEM((regions, members, 128), F32),
            dma((pieces + 1, 2, 20)),
            dma((pieces + 1, 2, 20)),
            dma((pieces, mems)),
            dma((pieces, mems)),
            dma((mems,)),
            dma((mems,)),
            dma((regions, mems)),
            dma((regions, mems)),
            dma((pieces + 1,)),
            dma(()),
            dma(()),
            *[pltpu.VMEM((blocks_dev * spaces, part, width), BF16) for _ in range(pieces)],
        ],
        compiler_params=pltpu.CompilerParams(
            vmem_limit_bytes=52 << 20, collective_id=0, has_side_effects=True
        ),
    )(block_list, block_count, loc_weight, ensemble_state, obs_ens, obs_prec, innovation, prior_weight)
    return jnp.transpose(updated, (1, 0, 2))


def solution(mesh):
    return jax.shard_map(
        body,
        mesh=mesh,
        in_specs=(
            P("mem", "space", None),
            P("mem", "space", None),
            P("space", None),
            P("space", None),
            P("space", None),
            P("space"),
            P("space", None),
            P("space", None),
        ),
        out_specs=P("mem", "space", None),
        check_vma=False,
    )
```

```python
import functools
import math

import jax
import jax.numpy as jnp
from jax import lax
from jax.experimental import pallas as pl
from jax.experimental.pallas import tpu as pltpu
from jax.sharding import PartitionSpec as P

INFLATION = 1.1
HIGHEST = lax.Precision.HIGHEST
F32 = jnp.float32
BF16 = jnp.bfloat16


def dot(a, b, dims, precision=None):
    return lax.dot_general(a, b, (dims, ((), ())), precision=precision, preferred_element_type=F32)


def split(x):
    high = x.astype(BF16)
    return high, (x - high.astype(F32)).astype(BF16)


def eliminate(rows, group, first):
    count = len(rows)
    rows = list(rows)

    def lane(x, i):
        return jnp.broadcast_to(x[:, first + i : first + i + 1], x.shape)

    for k in range(0, count, group):
        small = {(a, b): lane(rows[k + a], k + b) for a in range(group) for b in range(a, group)}
        for a in range(group):
            root = lax.rsqrt(small[a, a])
            upper = {b: small[a, b] * root for b in range(a + 1, group)}
            rows[k + a] = rows[k + a] * root
            for c in range(a + 1, group):
                rows[k + c] = rows[k + c] - upper[c] * rows[k + a]
                for b in range(c, group):
                    small[c, b] = small[c, b] - upper[c] * upper[b]
        for i in range(k + group, count):
            for a in range(group):
                rows[i] = rows[i] - lane(rows[k + a], i) * rows[k + a]
    return rows


def whole(
    list_ref, count_ref, loc_ref, state_ref, obs_hbm, prec_hbm, innov_hbm, prior_hbm,
    out_ref,
    listed, seen_obs, table, states_in, wide, result, seen, entry_rows, extra, system, diag, vectors, qcol,
    ring_send, ring_recv, obs_send, obs_recv, state_send, state_recv, out_send, out_recv, own_sem,
    table_send, table_recv, load_sem, obs_ref, given_ref, prior_ref,
    *blocks, side, nb, sub, group,
):
    pieces, mems, entries, part, width = seen_obs.shape
    members_dev, count = obs_ref.shape[:2]
    slots, rows_space = list_ref.shape
    regions = rows_space // mems
    members = mems * members_dev
    p_size = state_ref.shape[2]
    half = count // 2
    space, mem = lax.axis_index("space"), lax.axis_index("mem")
    core = mem % 2
    x, z = space // side, space % side
    first = mem * regions

    def at(axis, i, j):
        dx, dz = (i, j) if axis == 0 else (j, i)
        return (x + dx + side) % side * side + (z + dz + side) % side

    def peer(step):
        return (mem + step) % mems

    loads = [
        pltpu.make_async_copy(obs_hbm, obs_ref, load_sem.at[0]),
        pltpu.make_async_copy(prec_hbm, given_ref.at[0], load_sem.at[1]),
        pltpu.make_async_copy(innov_hbm, given_ref.at[1], load_sem.at[2]),
        pltpu.make_async_copy(prior_hbm, prior_ref, load_sem.at[3]),
    ]
    for load in loads:
        load.start()
    barrier = pltpu.get_barrier_semaphore()
    for there in [at(0, 1, 0), at(0, -1, 0), at(0, 0, 1), at(0, 0, -1)]:
        pl.semaphore_signal(barrier, inc=1, device_id={"space": there, "mem": mem})
    for step in range(1, mems):
        pl.semaphore_signal(barrier, inc=1, device_id={"space": space, "mem": peer(step)})

    def turn(p):
        for k in range(part):
            wide[0, k * count : (k + 1) * count, :] = obs_ref[p * part + k].astype(F32)

        def one(b, carry):
            block = wide[0, pl.ds(b, part, stride=count), :].astype(BF16)
            blocks[p][space * count + b] = block
            return carry

        lax.fori_loop(0, count, one, 0, unroll=8)

    loads[0].wait()
    turn(0)
    pl.semaphore_wait(barrier, 4 + mems - 1)

    rings = [*blocks, table.at[core]]

    def send(p, axis, number, chunk, share, to):
        start, size = {"all": (0, half), "low": (0, half // 2), "high": (half // 2, half // 2)}[share]
        rows = pl.ds(pl.multiple_of(chunk * count + start + axis * half, size), size)
        return pltpu.make_async_remote_copy(
            src_ref=rings[p].at[rows],
            dst_ref=rings[p].at[rows],
            send_sem=ring_send.at[p, axis, number],
            recv_sem=ring_recv.at[p, axis, number],
            device_id={"space": to, "mem": mem},
        )

    order = (0, -1, 1, 2)

    def copy_of(p, axis, number):
        if number == 0:
            return send(p, axis, 0, at(axis, 0, 0), "all", at(axis, 1, 0))
        if number == 1:
            return send(p, axis, 1, at(axis, 0, 0), "all", at(axis, -1, 0))
        if number == 2:
            return send(p, axis, 2, at(axis, -1, 0), "low", at(axis, 1, 0))
        if number == 3:
            return send(p, axis, 3, at(axis, 1, 0), "high", at(axis, -1, 0))
        d, kind = order[(number - 4) // 4], (number - 4) % 4
        if kind == 0:
            return send(p, axis, number, at(axis, d, 0), "all", at(axis, 0, 1))
        if kind == 1:
            return send(p, axis, number, at(axis, d, 0), "all", at(axis, 0, -1))
        if kind == 2:
            return send(p, axis, number, at(axis, d, -1), "low", at(axis, 0, 1))
        return send(p, axis, number, at(axis, d, 1), "high", at(axis, 0, -1))

    sent = []

    def start(p, *numbers):
        for number in numbers:
            for axis in (0, 1):
                copy = copy_of(p, axis, number)
                copy.start()
                sent.append(copy)

    def arrive(p, *numbers):
        for number in numbers:
            for axis in (0, 1):
                copy_of(p, axis, number).wait_recv()

    def begin(p):
        start(p, 0, 1, 4, 5)

    def spread(p):
        arrive(p, 0)
        start(p, 2, 8, 9)
        arrive(p, 1)
        start(p, 3, 12, 13)
        arrive(p, 2, 3)
        start(p, 16, 17)

    def hand_on(p):
        for j in range(4):
            for kind in (0, 1):
                arrive(p, 4 + 4 * j + kind)
                start(p, 4 + 4 * j + kind + 2)

    def gathered(p):
        for j in range(4):
            arrive(p, 6 + 4 * j, 7 + 4 * j)

    def state_copy(step):
        to = peer(step)
        return pltpu.make_async_remote_copy(
            src_ref=state_ref.at[:, pl.ds(pl.multiple_of(to * regions, regions), regions), :],
            dst_ref=states_in.at[mem],
            send_sem=state_send.at[step],
            recv_sem=state_recv.at[step],
            device_id={"space": space, "mem": to},
        )

    def obs_copy(p, step):
        to = peer(step)
        return pltpu.make_async_remote_copy(
            src_ref=listed.at[p, pl.ds(pl.multiple_of(to * entries, entries), entries)],
            dst_ref=seen_obs.at[p, mem],
            send_sem=obs_send.at[p, step],
            recv_sem=obs_recv.at[p, step],
            device_id={"space": space, "mem": to},
        )

    local = []

    def begin_states():
        copy = pltpu.make_async_copy(
            state_ref.at[:, pl.ds(pl.multiple_of(first, regions), regions), :],
            states_in.at[mem],
            own_sem.at[pieces],
        )
        copy.start()
        local.append(copy)
        for step in range(1, mems):
            state_copy(step).start()

    begin(0)
    for p in range(1, pieces):
        turn(p)
    for load in loads[1:]:
        load.wait()
    here = pl.ds(pl.multiple_of(space * count, count), count)
    table[core, here, :] = jnp.where(core == 0, given_ref[0], given_ref[1])
    spread(0)
    begin(1)
    for p in range(pieces):
        hand_on(p)
        if p + 1 < pieces:
            spread(p + 1)
        if p + 1 < pieces:
            begin(p + 2 if p + 2 < pieces else pieces)
        gathered(p)

        def pick(r, carry, p=p):
            for l in range(slots):
                listed[p, r * slots + l] = blocks[p][list_ref[l, r]]
            return carry

        lax.fori_loop(0, rows_space, pick, 0, unroll=4)
        mine = pltpu.make_async_copy(
            listed.at[p, pl.ds(pl.multiple_of(mem * entries, entries), entries)],
            seen_obs.at[p, mem],
            own_sem.at[p],
        )
        mine.start()
        local.append(mine)
        for step in range(1, mems):
            obs_copy(p, step).start()

    begin_states()
    extra[...] = jnp.zeros_like(extra)
    shares_all = prior_ref[pl.ds(pl.multiple_of(first, regions), regions), :]
    shares_all = shares_all / jnp.sum(shares_all, axis=1, keepdims=True)
    root_t = jnp.transpose(jnp.sqrt(members * shares_all))
    for r in range(regions):
        qcol[r] = jnp.broadcast_to(root_t[:, r : r + 1], (members, 128))
    halves = members // 128
    spread(pieces)
    hand_on(pieces)
    gathered(pieces)
    other = pltpu.make_async_remote_copy(
        src_ref=table.at[core],
        dst_ref=table.at[core],
        send_sem=table_send,
        recv_sem=table_recv,
        device_id={"space": space, "mem": mem + 1 - 2 * core},
    )
    other.start()
    other.wait()

    def fetch(r, carry):
        row = first + r
        for l in range(slots):
            block = list_ref[l, row]
            live = jnp.where(l < count_ref[row], loc_ref[l, row], 0.0)
            entry_rows[0, pl.ds(r * slots + l, 1), :] = live * table[0, pl.ds(block, 1), :]
            entry_rows[1, pl.ds(r * slots + l, 1), :] = table[1, pl.ds(block, 1), :]
        return carry

    lax.fori_loop(0, regions, fetch, 0)
    entry_rows[0] = jnp.sqrt(entry_rows[0])
    entry_rows[1] = entry_rows[0] * entry_rows[1]
    for copy in sent:
        copy.wait_send()
    for p in range(0, pieces, 2):
        for which in (p, p + 1):
            local[which].wait()
            for step in range(1, mems):
                obs_copy(which, step).wait()

        def weigh(r, carry, p=p):
            for l in range(slots):
                scale = entry_rows[0, pl.ds(r * slots + l, 1), :]
                for m in range(mems):
                    picked = jnp.concatenate(
                        [seen_obs[p, m, r * slots + l], seen_obs[p + 1, m, r * slots + l]], axis=0
                    ).astype(F32)
                    at_m = slice(m * members_dev + p * part, m * members_dev + (p + 2) * part)
                    seen[r, at_m, l * width : (l + 1) * width] = (picked * scale).astype(BF16)
            return carry

        lax.fori_loop(0, regions, weigh, 0, unroll=2)

    row_id = lax.broadcasted_iota(jnp.int32, (members, members), 0)
    col_id = lax.broadcasted_iota(jnp.int32, (members, members), 1)

    def shares_of(r):
        s = prior_ref[pl.ds(first + r, 1), :]
        return s / jnp.sum(s, axis=1, keepdims=True)

    def build(r, carry):
        for l in range(slots):
            cols = slice(l * width, (l + 1) * width)
            high, low = split(entry_rows[1, pl.ds(r * slots + l, 1), :])
            extra[0:1, cols] = high.astype(F32)
            extra[1:2, cols] = low.astype(F32)
        all_seen = seen[r]
        gram = dot(all_seen, all_seen, ((1,), (1,)))
        proj = dot(extra[...].astype(BF16), all_seen, ((1,), (1,)))
        proj = proj[0:1] + proj[1:2]
        shares = shares_of(r)
        root = jnp.sqrt(members * shares)
        left = dot(jnp.broadcast_to(shares, (8, members)), gram, ((1,), (0,)), HIGHEST)[0:1]
        centred = gram - left
        centred = centred - jnp.sum(centred * shares, axis=1, keepdims=True)
        q = jnp.concatenate([qcol[r]] * halves, axis=1)
        full = q * centred * root + jnp.where(row_id == col_id, (members - 1) / INFLATION, 0.0)
        at_r = pl.ds(pl.multiple_of(r * members, members), members)
        for h in range(halves):
            system[h, at_r, :] = full[:, h * 128 : (h + 1) * 128]
        vectors[pl.ds(r, 1), :] = root * (proj - jnp.sum(shares * proj, axis=1, keepdims=True))
        return carry

    lax.fori_loop(0, regions, build, 0, unroll=2)

    def take_states():
        for step in range(1, mems):
            state_copy(step).wait()
        local[-1].wait()
        for m in range(mems):
            many = states_in[m].astype(F32).reshape(members_dev * regions, p_size)
            for h in range(p_size // 128):
                wide[h, m * members_dev * regions : (m + 1) * members_dev * regions, :] = many[
                    :, h * 128 : (h + 1) * 128
                ]

    lane_id = lax.broadcasted_iota(jnp.int32, (regions, 128), 1)
    for b in range(members // nb):
        h_b, place = b * nb // 128, b * nb % 128
        if b == members // nb // 2:
            take_states()
        for part_b in range(0, nb, sub):
            if part_b == 0:
                rows = []
                for i in range(sub):
                    row = system[h_b, pl.ds(b * nb + i, regions, stride=members), :]
                    if place:
                        row = pltpu.roll(row, 128 - place, 1)
                    rows.append(jnp.where(lane_id < nb, row, jnp.where(lane_id == nb + i, 1.0, 0.0)))
            else:
                rows = [diag[pl.ds(part_b + i, regions, stride=nb), :] for i in range(sub)]
            rows = eliminate(rows, group, part_b)
            for i in range(sub):
                diag[pl.ds(part_b + i, regions, stride=nb), :] = rows[i]
            if part_b:
                continue
            for r in range(regions):
                ready = diag[r * nb : r * nb + sub, :]
                later = system[h_b, r * members + b * nb + sub : r * members + (b + 1) * nb, :]
                if place:
                    later = pltpu.roll(later, 128 - place, 1)
                lanes = lax.broadcasted_iota(jnp.int32, (nb - sub, 128), 1)
                which = lax.broadcasted_iota(jnp.int32, (nb - sub, 128), 0)
                later = jnp.where(lanes < nb, later, jnp.where(lanes == nb + sub + which, 1.0, 0.0))
                later = later - dot(ready[:, sub:nb], ready, ((0,), (0,)), HIGHEST)
                diag[r * nb + sub : (r + 1) * nb, :] = later

        def sweep(r, carry, b=b, h_b=h_b, place=place):
            begins = r * members + b * nb
            band_rows = pl.ds(pl.multiple_of(begins, nb), nb)
            small = diag[pl.ds(pl.multiple_of(r * nb, nb), nb), :][:, nb : 2 * nb]
            band = jnp.concatenate([system[h, band_rows, :] for h in range(halves)], axis=1)
            ids = lax.broadcasted_iota(jnp.int32, (nb, members), 1)
            rid = lax.broadcasted_iota(jnp.int32, (nb, members), 0)
            mine = (ids >= b * nb) & (ids < (b + 1) * nb)
            band = jnp.where(mine, jnp.where(ids - b * nb == rid, 1.0, 0.0), band)
            done = dot(small, band, ((1,), (0,)), HIGHEST)
            kept = jnp.where(ids < (b + 1) * nb, done, 0.0)
            for h in range(halves):
                system[h, band_rows, :] = kept[:, h * 128 : (h + 1) * 128]
            rest = members - (b + 1) * nb
            if rest:
                below = pl.ds(pl.multiple_of(begins + nb, nb), rest)
                change = dot(done[:, (b + 1) * nb :], done, ((0,), (0,)), HIGHEST)
                for h in range(halves):
                    old = system[h, below, :]
                    if h == h_b:
                        lanes = lax.broadcasted_iota(jnp.int32, (rest, 128), 1)
                        old = jnp.where((lanes >= place) & (lanes < place + nb), 0.0, old)
                    system[h, below, :] = old - change[:, h * 128 : (h + 1) * 128]
            return carry

        lax.fori_loop(0, regions, sweep, 0, unroll=True)

    def out_copy(r, step):
        to = peer(step)
        return pltpu.make_async_remote_copy(
            src_ref=result.at[r, pl.ds(pl.multiple_of(to * members_dev, members_dev), members_dev), :],
            dst_ref=out_ref.at[first + r],
            send_sem=out_send.at[r, step],
            recv_sem=out_recv.at[r, step],
            device_id={"space": space, "mem": to},
        )

    def own_out(r):
        return pltpu.make_async_copy(
            result.at[r, pl.ds(pl.multiple_of(mem * members_dev, members_dev), members_dev), :],
            out_ref.at[first + r],
            out_send.at[r, 0],
        )

    def finish(r, carry):
        at_r = pl.ds(pl.multiple_of(r * members, members), members)
        inverse = jnp.concatenate([system[h, at_r, :] for h in range(halves)], axis=1)
        shares = shares_of(r)
        root = jnp.sqrt(members * shares)
        solved = jnp.sum(inverse * vectors[pl.ds(r, 1), :], axis=1, keepdims=True)
        weights = jnp.sum(inverse * solved, axis=0, keepdims=True)
        mixing = root * (weights + math.sqrt(members - 1.0) * inverse)
        mixing = mixing - jnp.sum(mixing, axis=1, keepdims=True) * shares + shares
        high, low = split(mixing)
        states = jnp.concatenate(
            [wide[h, pl.ds(r, members, stride=regions), :] for h in range(p_size // 128)], axis=1
        ).astype(BF16)
        done = dot(high, states, ((1,), (0,))) + dot(low, states, ((1,), (0,)))
        result[r] = done.astype(BF16)
        own_out(r).start()
        for step in range(1, mems):
            out_copy(r, step).start()
        return carry

    lax.fori_loop(0, regions, finish, 0, unroll=2)

    def close(r, carry):
        own_out(r).wait()
        for step in range(1, mems):
            out_copy(r, step).wait()
        return carry

    lax.fori_loop(0, regions, close, 0)


SMEM = pl.BlockSpec(memory_space=pltpu.SMEM)
VMEM = pl.BlockSpec(memory_space=pltpu.VMEM)
HBM = pl.BlockSpec(memory_space=pltpu.HBM)


def body(
    ensemble_state, obs_ens, innovation, obs_prec, block_list, block_count, loc_weight, prior_weight
):
    spaces, mems = lax.axis_size("space"), lax.axis_size("mem")
    members_dev, regions_dev, p_size = ensemble_state.shape
    blocks_dev, width = obs_ens.shape[1:]
    slots = block_list.shape[1]
    regions = regions_dev // mems
    entries = regions * slots
    members = members_dev * mems
    pieces = 4
    part = members_dev // pieces
    nb = 64
    dma = pltpu.SemaphoreType.DMA
    updated = pl.pallas_call(
        functools.partial(whole, side=math.isqrt(spaces), nb=nb, sub=32, group=8),
        in_specs=[SMEM, SMEM, SMEM, HBM, HBM, HBM, HBM, HBM],
        out_specs=VMEM,
        out_shape=jax.ShapeDtypeStruct((regions_dev, members_dev, p_size), BF16),
        scratch_shapes=[
            pltpu.VMEM((pieces, regions_dev * slots, part, width), BF16),
            pltpu.VMEM((pieces, mems, entries, part, width), BF16),
            pltpu.VMEM((2, blocks_dev * spaces, width), F32),
            pltpu.VMEM((mems, members_dev, regions, p_size), BF16),
            pltpu.VMEM((p_size // 128, max(members * regions, members_dev * blocks_dev), 128), F32),
            pltpu.VMEM((regions, members, p_size), BF16),
            pltpu.VMEM((regions, members, slots * width), BF16),
            pltpu.VMEM((2, entries, width), F32),
            pltpu.VMEM((16, slots * width), F32),
            pltpu.VMEM((members // 128, regions * members, 128), F32),
            pltpu.VMEM((regions * nb, 128), F32),
            pltpu.VMEM((regions, members), F32),
            pltpu.VMEM((regions, members, 128), F32),
            dma((pieces + 1, 2, 20)),
            dma((pieces + 1, 2, 20)),
            dma((pieces, mems)),
            dma((pieces, mems)),
            dma((mems,)),
            dma((mems,)),
            dma((regions, mems)),
            dma((regions, mems)),
            dma((pieces + 1,)),
            dma(()),
            dma(()),
            dma((4,)),
            pltpu.VMEM((members_dev, blocks_dev, width), BF16),
            pltpu.VMEM((2, blocks_dev, width), F32),
            pltpu.VMEM((regions_dev, members), F32),
            *[pltpu.VMEM((blocks_dev * spaces, part, width), BF16) for _ in range(pieces)],
        ],
        compiler_params=pltpu.CompilerParams(
            vmem_limit_bytes=63 << 20, collective_id=0, has_side_effects=True
        ),
    )(
        block_list.T, block_count, loc_weight.T,
        ensemble_state, obs_ens, obs_prec, innovation, prior_weight,
    )
    return jnp.transpose(updated, (1, 0, 2))


def solution(mesh):
    return jax.shard_map(
        body,
        mesh=mesh,
        in_specs=(
            P("mem", "space", None),
            P("mem", "space", None),
            P("space", None),
            P("space", None),
            P("space", None),
            P("space"),
            P("space", None),
            P("space", None),
        ),
        out_specs=P("mem", "space", None),
        check_vma=False,
    )
```

```python
import functools
import math

import jax
import jax.numpy as jnp
from jax import lax
from jax.experimental import pallas as pl
from jax.experimental.pallas import tpu as pltpu
from jax.sharding import PartitionSpec as P

INFLATION = 1.1
HIGHEST = lax.Precision.HIGHEST
F32 = jnp.float32
BF16 = jnp.bfloat16


def dot(a, b, dims, precision=None):
    return lax.dot_general(a, b, (dims, ((), ())), precision=precision, preferred_element_type=F32)


def split(x):
    high = x.astype(BF16)
    return high, (x - high.astype(F32)).astype(BF16)


def eliminate(rows, group, first):
    count = len(rows)
    rows = list(rows)

    def lane(x, i):
        return jnp.broadcast_to(x[:, first + i : first + i + 1], x.shape)

    for k in range(0, count, group):
        small = {(a, b): lane(rows[k + a], k + b) for a in range(group) for b in range(a, group)}
        for a in range(group):
            root = lax.rsqrt(small[a, a])
            upper = {b: small[a, b] * root for b in range(a + 1, group)}
            rows[k + a] = rows[k + a] * root
            for c in range(a + 1, group):
                rows[k + c] = rows[k + c] - upper[c] * rows[k + a]
                for b in range(c, group):
                    small[c, b] = small[c, b] - upper[c] * upper[b]
        for i in range(k + group, count):
            for a in range(group):
                rows[i] = rows[i] - lane(rows[k + a], i) * rows[k + a]
    return rows


def whole(
    list_ref, count_ref, loc_ref, state_ref, obs_hbm, prec_hbm, innov_hbm, prior_hbm,
    out_ref,
    listed, seen_obs, table, states_in, wide, result, seen, entry_rows, picked_rows, given_rows, extra, system, diag, vectors, qcol,
    ring_send, ring_recv, obs_send, obs_recv, state_send, state_recv, out_send, out_recv, own_sem,
    table_send, table_recv, load_sem, obs_ref, given_ref, prior_ref,
    *blocks, side, nb, sub, group,
):
    pieces, mems, entries, part, width = seen_obs.shape
    members_dev, count = obs_ref.shape[:2]
    slots, rows_space = list_ref.shape
    regions = rows_space // mems
    members = mems * members_dev
    p_size = state_ref.shape[2]
    half = count // 2
    space, mem = lax.axis_index("space"), lax.axis_index("mem")
    core = mem % 2
    x, z = space // side, space % side
    first = mem * regions

    def at(axis, i, j):
        dx, dz = (i, j) if axis == 0 else (j, i)
        return (x + dx + side) % side * side + (z + dz + side) % side

    def peer(step):
        return (mem // 2 + step // 2) % (mems // 2) * 2 + (core + step % 2) % 2

    loads = [
        pltpu.make_async_copy(obs_hbm, obs_ref, load_sem.at[0]),
        pltpu.make_async_copy(prec_hbm, given_ref.at[0], load_sem.at[1]),
        pltpu.make_async_copy(innov_hbm, given_ref.at[1], load_sem.at[2]),
        pltpu.make_async_copy(prior_hbm, prior_ref, load_sem.at[3]),
    ]
    for load in loads:
        load.start()
    barrier = pltpu.get_barrier_semaphore()
    for there in [at(0, 1, 0), at(0, -1, 0), at(0, 0, 1), at(0, 0, -1)]:
        pl.semaphore_signal(barrier, inc=1, device_id={"space": there, "mem": mem})
    for step in range(1, mems):
        pl.semaphore_signal(barrier, inc=1, device_id={"space": space, "mem": peer(step)})

    def turn(p):
        for k in range(part):
            wide[0, k * count : (k + 1) * count, :] = obs_ref[p * part + k].astype(F32)

        def one(b, carry):
            block = wide[0, pl.ds(b, part, stride=count), :].astype(BF16)
            blocks[p][space * count + b] = block
            return carry

        lax.fori_loop(0, count, one, 0, unroll=8)

    loads[0].wait()
    turn(0)
    pl.semaphore_wait(barrier, 4 + mems - 1)

    rings = [*blocks, table]

    def send(p, axis, number, chunk, share, to):
        start, size = {"all": (0, half), "low": (0, half // 2), "high": (half // 2, half // 2)}[share]
        rows = pl.ds(pl.multiple_of(chunk * count + start + axis * half, size), size)
        return pltpu.make_async_remote_copy(
            src_ref=rings[p].at[rows],
            dst_ref=rings[p].at[rows],
            send_sem=ring_send.at[p, axis, number],
            recv_sem=ring_recv.at[p, axis, number],
            device_id={"space": to, "mem": mem},
        )

    order = (0, -1, 1, 2)

    def copy_of(p, axis, number):
        if number == 0:
            return send(p, axis, 0, at(axis, 0, 0), "all", at(axis, 1, 0))
        if number == 1:
            return send(p, axis, 1, at(axis, 0, 0), "all", at(axis, -1, 0))
        if number == 2:
            return send(p, axis, 2, at(axis, -1, 0), "low", at(axis, 1, 0))
        if number == 3:
            return send(p, axis, 3, at(axis, 1, 0), "high", at(axis, -1, 0))
        d, kind = order[(number - 4) // 4], (number - 4) % 4
        if kind == 0:
            return send(p, axis, number, at(axis, d, 0), "all", at(axis, 0, 1))
        if kind == 1:
            return send(p, axis, number, at(axis, d, 0), "all", at(axis, 0, -1))
        if kind == 2:
            return send(p, axis, number, at(axis, d, -1), "low", at(axis, 0, 1))
        return send(p, axis, number, at(axis, d, 1), "high", at(axis, 0, -1))

    sent = []

    def start(p, *numbers):
        for number in numbers:
            for axis in (0, 1):
                copy = copy_of(p, axis, number)
                copy.start()
                sent.append(copy)

    def arrive(p, *numbers):
        for number in numbers:
            for axis in (0, 1):
                copy_of(p, axis, number).wait_recv()

    def begin(p):
        start(p, 0, 1, 4, 5)

    def spread(p):
        arrive(p, 0)
        start(p, 2, 8, 9)
        arrive(p, 1)
        start(p, 3, 12, 13)
        arrive(p, 2, 3)
        start(p, 16, 17)

    def hand_on(p):
        for j in range(4):
            for kind in (0, 1):
                arrive(p, 4 + 4 * j + kind)
                start(p, 4 + 4 * j + kind + 2)

    def gathered(p):
        for j in range(4):
            arrive(p, 6 + 4 * j, 7 + 4 * j)

    def state_copy(step):
        to = peer(step)
        return pltpu.make_async_remote_copy(
            src_ref=state_ref.at[:, pl.ds(pl.multiple_of(to * regions, regions), regions), :],
            dst_ref=states_in.at[mem],
            send_sem=state_send.at[step],
            recv_sem=state_recv.at[step],
            device_id={"space": space, "mem": to},
        )

    def obs_copy(p, step):
        to = peer(step)
        return pltpu.make_async_remote_copy(
            src_ref=listed.at[p, pl.ds(pl.multiple_of(to * entries, entries), entries)],
            dst_ref=seen_obs.at[p, mem],
            send_sem=obs_send.at[p, step],
            recv_sem=obs_recv.at[p, step],
            device_id={"space": space, "mem": to},
        )

    local = []

    def begin_states():
        copy = pltpu.make_async_copy(
            state_ref.at[:, pl.ds(pl.multiple_of(first, regions), regions), :],
            states_in.at[mem],
            own_sem.at[pieces],
        )
        copy.start()
        local.append(copy)
        for step in range(1, mems):
            state_copy(step).start()

    begin(0)
    begin_states()
    local_states = local.pop()
    for p in range(1, pieces):
        turn(p)
    for load in loads[1:]:
        load.wait()
    here = pl.ds(pl.multiple_of(space * count, count), count)
    table[here, :] = jnp.where(core == 0, given_ref[0], given_ref[1])
    spread(0)
    begin(1)
    for p in range(pieces):
        hand_on(p)
        if p + 1 < pieces:
            spread(p + 1)
        if p + 1 < pieces:
            begin(p + 2 if p + 2 < pieces else pieces)
        else:
            spread(pieces)
        gathered(p)

        for step in sorted(range(mems), key=lambda k: (k == 0, k == 1, k // 2 != mems // 4)):
            to = peer(step)

            def pick(r, carry, p=p, to=to):
                row = to * regions + r
                for l in range(slots):
                    listed[p, row * slots + l] = blocks[p][list_ref[l, row]]
                return carry

            lax.fori_loop(0, regions, pick, 0, unroll=4)
            if step:
                obs_copy(p, step).start()
        mine = pltpu.make_async_copy(
            listed.at[p, pl.ds(pl.multiple_of(mem * entries, entries), entries)],
            seen_obs.at[p, mem],
            own_sem.at[p],
        )
        mine.start()
        local.append(mine)

    extra[...] = jnp.zeros_like(extra)
    shares_all = prior_ref[pl.ds(pl.multiple_of(first, regions), regions), :]
    shares_all = shares_all / jnp.sum(shares_all, axis=1, keepdims=True)
    root_t = jnp.transpose(jnp.sqrt(members * shares_all))
    for r in range(regions):
        qcol[r] = jnp.broadcast_to(root_t[:, r : r + 1], (members, 128))
    halves = members // 128
    hand_on(pieces)
    gathered(pieces)
    def pick_rows(r, carry):
        for c in range(2):
            for l in range(slots):
                block = list_ref[l, (mem - core + c) * regions + r]
                picked_rows[c, pl.ds(r * slots + l, 1), :] = table[pl.ds(block, 1), :]
        return carry

    lax.fori_loop(0, regions, pick_rows, 0, unroll=2)
    other = pltpu.make_async_remote_copy(
        src_ref=picked_rows.at[1 - core],
        dst_ref=given_rows.at[core],
        send_sem=table_send,
        recv_sem=table_recv,
        device_id={"space": space, "mem": mem + 1 - 2 * core},
    )
    other.start()
    given_rows[core] = picked_rows[core]
    other.wait()

    def fetch(r, carry):
        row = first + r
        for l in range(slots):
            at_e = pl.ds(r * slots + l, 1)
            live = jnp.where(l < count_ref[row], loc_ref[l, row], 0.0)
            entry_rows[0, at_e, :] = live * given_rows[0, at_e, :]
        return carry

    lax.fori_loop(0, regions, fetch, 0)
    entry_rows[0] = jnp.sqrt(entry_rows[0])
    entry_rows[1] = entry_rows[0] * given_rows[1]
    for copy in sent:
        copy.wait_send()
    for p in range(0, pieces, 2):
        for which in (p, p + 1):
            local[which].wait()
            for step in range(1, mems):
                obs_copy(which, step).wait()

        def weigh(r, carry, p=p):
            for l in range(slots):
                scale = entry_rows[0, pl.ds(r * slots + l, 1), :]
                for m in range(mems):
                    picked = jnp.concatenate(
                        [seen_obs[p, m, r * slots + l], seen_obs[p + 1, m, r * slots + l]], axis=0
                    ).astype(F32)
                    at_m = slice(m * members_dev + p * part, m * members_dev + (p + 2) * part)
                    seen[r, at_m, l * width : (l + 1) * width] = (picked * scale).astype(BF16)
            return carry

        lax.fori_loop(0, regions, weigh, 0, unroll=2)

    row_id = lax.broadcasted_iota(jnp.int32, (members, members), 0)
    col_id = lax.broadcasted_iota(jnp.int32, (members, members), 1)

    def shares_of(r):
        s = prior_ref[pl.ds(first + r, 1), :]
        return s / jnp.sum(s, axis=1, keepdims=True)

    def build(r, carry):
        for l in range(slots):
            cols = slice(l * width, (l + 1) * width)
            high, low = split(entry_rows[1, pl.ds(r * slots + l, 1), :])
            extra[0:1, cols] = high.astype(F32)
            extra[1:2, cols] = low.astype(F32)
        all_seen = seen[r]
        gram = dot(all_seen, all_seen, ((1,), (1,)))
        proj = dot(extra[...].astype(BF16), all_seen, ((1,), (1,)))
        proj = proj[0:1] + proj[1:2]
        shares = shares_of(r)
        root = jnp.sqrt(members * shares)
        left = dot(jnp.broadcast_to(shares, (8, members)), gram, ((1,), (0,)), HIGHEST)[0:1]
        centred = gram - left
        centred = centred - jnp.sum(centred * shares, axis=1, keepdims=True)
        q = jnp.concatenate([qcol[r]] * halves, axis=1)
        full = q * centred * root + jnp.where(row_id == col_id, (members - 1) / INFLATION, 0.0)
        at_r = pl.ds(pl.multiple_of(r * members, members), members)
        for h in range(halves):
            system[h, at_r, :] = full[:, h * 128 : (h + 1) * 128]
        vectors[pl.ds(r, 1), :] = root * (proj - jnp.sum(shares * proj, axis=1, keepdims=True))
        return carry

    lax.fori_loop(0, regions, build, 0, unroll=4)

    def take_states():
        for step in range(1, mems):
            state_copy(step).wait()
        local_states.wait()
        for m in range(mems):
            many = states_in[m].astype(F32).reshape(members_dev * regions, p_size)
            for h in range(p_size // 128):
                wide[h, m * members_dev * regions : (m + 1) * members_dev * regions, :] = many[
                    :, h * 128 : (h + 1) * 128
                ]

    lane_id = lax.broadcasted_iota(jnp.int32, (regions, 128), 1)
    for b in range(members // nb):
        h_b, place = b * nb // 128, b * nb % 128
        if b == members // nb // 2:
            take_states()
        for part_b in range(0, nb, sub):
            if part_b == 0:
                rows = []
                for i in range(sub):
                    row = system[h_b, pl.ds(b * nb + i, regions, stride=members), :]
                    if place:
                        row = pltpu.roll(row, 128 - place, 1)
                    rows.append(jnp.where(lane_id < nb, row, jnp.where(lane_id == nb + i, 1.0, 0.0)))
            else:
                rows = [diag[pl.ds(part_b + i, regions, stride=nb), :] for i in range(sub)]
            rows = eliminate(rows, group, part_b)
            for i in range(sub):
                diag[pl.ds(part_b + i, regions, stride=nb), :] = rows[i]
            if part_b:
                continue
            for r in range(regions):
                ready = diag[r * nb : r * nb + sub, :]
                later = system[h_b, r * members + b * nb + sub : r * members + (b + 1) * nb, :]
                if place:
                    later = pltpu.roll(later, 128 - place, 1)
                lanes = lax.broadcasted_iota(jnp.int32, (nb - sub, 128), 1)
                which = lax.broadcasted_iota(jnp.int32, (nb - sub, 128), 0)
                later = jnp.where(lanes < nb, later, jnp.where(lanes == nb + sub + which, 1.0, 0.0))
                later = later - dot(ready[:, sub:nb], ready, ((0,), (0,)), HIGHEST)
                diag[r * nb + sub : (r + 1) * nb, :] = later

        def sweep(r, carry, b=b, h_b=h_b, place=place):
            begins = r * members + b * nb
            band_rows = pl.ds(pl.multiple_of(begins, nb), nb)
            small = diag[pl.ds(pl.multiple_of(r * nb, nb), nb), :][:, nb : 2 * nb]
            band = jnp.concatenate([system[h, band_rows, :] for h in range(halves)], axis=1)
            ids = lax.broadcasted_iota(jnp.int32, (nb, members), 1)
            rid = lax.broadcasted_iota(jnp.int32, (nb, members), 0)
            mine = (ids >= b * nb) & (ids < (b + 1) * nb)
            band = jnp.where(mine, jnp.where(ids - b * nb == rid, 1.0, 0.0), band)
            done = dot(small, band, ((1,), (0,)), HIGHEST)
            kept = jnp.where(ids < (b + 1) * nb, done, 0.0)
            for h in range(halves):
                system[h, band_rows, :] = kept[:, h * 128 : (h + 1) * 128]
            rest = members - (b + 1) * nb
            if rest:
                below = pl.ds(pl.multiple_of(begins + nb, nb), rest)
                change = dot(done[:, (b + 1) * nb :], done, ((0,), (0,)), HIGHEST)
                for h in range(halves):
                    old = system[h, below, :]
                    if h == h_b:
                        lanes = lax.broadcasted_iota(jnp.int32, (rest, 128), 1)
                        old = jnp.where((lanes >= place) & (lanes < place + nb), 0.0, old)
                    system[h, below, :] = old - change[:, h * 128 : (h + 1) * 128]
            return carry

        lax.fori_loop(0, regions, sweep, 0, unroll=True)

    def out_copy(r, step):
        to = peer(step)
        return pltpu.make_async_remote_copy(
            src_ref=result.at[r, pl.ds(pl.multiple_of(to * members_dev, members_dev), members_dev), :],
            dst_ref=out_ref.at[first + r],
            send_sem=out_send.at[r, step],
            recv_sem=out_recv.at[r, step],
            device_id={"space": space, "mem": to},
        )

    def own_out(r):
        return pltpu.make_async_copy(
            result.at[r, pl.ds(pl.multiple_of(mem * members_dev, members_dev), members_dev), :],
            out_ref.at[first + r],
            out_send.at[r, 0],
        )

    def finish(r, carry):
        at_r = pl.ds(pl.multiple_of(r * members, members), members)
        inverse = jnp.concatenate([system[h, at_r, :] for h in range(halves)], axis=1)
        shares = shares_of(r)
        root = jnp.sqrt(members * shares)
        solved = jnp.sum(inverse * vectors[pl.ds(r, 1), :], axis=1, keepdims=True)
        weights = jnp.sum(inverse * solved, axis=0, keepdims=True)
        mixing = root * (weights + math.sqrt(members - 1.0) * inverse)
        mixing = mixing - jnp.sum(mixing, axis=1, keepdims=True) * shares + shares
        high, low = split(mixing)
        states = jnp.concatenate(
            [wide[h, pl.ds(r, members, stride=regions), :] for h in range(p_size // 128)], axis=1
        ).astype(BF16)
        done = dot(high, states, ((1,), (0,))) + dot(low, states, ((1,), (0,)))
        result[r] = done.astype(BF16)
        own_out(r).start()
        for step in range(1, mems):
            out_copy(r, step).start()
        return carry

    lax.fori_loop(0, regions, finish, 0, unroll=4)

    def close(r, carry):
        own_out(r).wait()
        for step in range(1, mems):
            out_copy(r, step).wait()
        return carry

    lax.fori_loop(0, regions, close, 0)


SMEM = pl.BlockSpec(memory_space=pltpu.SMEM)
VMEM = pl.BlockSpec(memory_space=pltpu.VMEM)
HBM = pl.BlockSpec(memory_space=pltpu.HBM)


def body(
    ensemble_state, obs_ens, innovation, obs_prec, block_list, block_count, loc_weight, prior_weight
):
    spaces, mems = lax.axis_size("space"), lax.axis_size("mem")
    members_dev, regions_dev, p_size = ensemble_state.shape
    blocks_dev, width = obs_ens.shape[1:]
    slots = block_list.shape[1]
    regions = regions_dev // mems
    entries = regions * slots
    members = members_dev * mems
    pieces = 4
    part = members_dev // pieces
    nb = 64
    dma = pltpu.SemaphoreType.DMA
    updated = pl.pallas_call(
        functools.partial(whole, side=math.isqrt(spaces), nb=nb, sub=32, group=8),
        in_specs=[SMEM, SMEM, SMEM, HBM, HBM, HBM, HBM, HBM],
        out_specs=VMEM,
        out_shape=jax.ShapeDtypeStruct((regions_dev, members_dev, p_size), BF16),
        scratch_shapes=[
            pltpu.VMEM((pieces, regions_dev * slots, part, width), BF16),
            pltpu.VMEM((pieces, mems, entries, part, width), BF16),
            pltpu.VMEM((blocks_dev * spaces, width), F32),
            pltpu.VMEM((mems, members_dev, regions, p_size), BF16),
            pltpu.VMEM((p_size // 128, max(members * regions, members_dev * blocks_dev), 128), F32),
            pltpu.VMEM((regions, members, p_size), BF16),
            pltpu.VMEM((regions, members, slots * width), BF16),
            pltpu.VMEM((2, entries, width), F32),
            pltpu.VMEM((2, entries, width), F32),
            pltpu.VMEM((2, entries, width), F32),
            pltpu.VMEM((16, slots * width), F32),
            pltpu.VMEM((members // 128, regions * members, 128), F32),
            pltpu.VMEM((regions * nb, 128), F32),
            pltpu.VMEM((regions, members), F32),
            pltpu.VMEM((regions, members, 128), F32),
            dma((pieces + 1, 2, 20)),
            dma((pieces + 1, 2, 20)),
            dma((pieces, mems)),
            dma((pieces, mems)),
            dma((mems,)),
            dma((mems,)),
            dma((regions, mems)),
            dma((regions, mems)),
            dma((pieces + 1,)),
            dma(()),
            dma(()),
            dma((4,)),
            pltpu.VMEM((members_dev, blocks_dev, width), BF16),
            pltpu.VMEM((2, blocks_dev, width), F32),
            pltpu.VMEM((regions_dev, members), F32),
            *[pltpu.VMEM((blocks_dev * spaces, part, width), BF16) for _ in range(pieces)],
        ],
        compiler_params=pltpu.CompilerParams(
            vmem_limit_bytes=63 << 20, collective_id=0, has_side_effects=True
        ),
    )(
        block_list.T, block_count, loc_weight.T,
        ensemble_state, obs_ens, obs_prec, innovation, prior_weight,
    )
    return jnp.transpose(updated, (1, 0, 2))


def solution(mesh):
    return jax.shard_map(
        body,
        mesh=mesh,
        in_specs=(
            P("mem", "space", None),
            P("mem", "space", None),
            P("space", None),
            P("space", None),
            P("space", None),
            P("space"),
            P("space", None),
            P("space", None),
        ),
        out_specs=P("mem", "space", None),
        check_vma=False,
    )
```

```python
import functools
import math

import jax
import jax.numpy as jnp
from jax import lax
from jax.experimental import pallas as pl
from jax.experimental.pallas import tpu as pltpu
from jax.sharding import PartitionSpec as P

INFLATION = 1.1
HIGHEST = lax.Precision.HIGHEST
F32 = jnp.float32
BF16 = jnp.bfloat16


def dot(a, b, dims, precision=None):
    return lax.dot_general(a, b, (dims, ((), ())), precision=precision, preferred_element_type=F32)


def split(x):
    high = x.astype(BF16)
    return high, (x - high.astype(F32)).astype(BF16)


def eliminate(rows, group, first):
    count = len(rows)
    rows = list(rows)

    def lane(x, i):
        return jnp.broadcast_to(x[:, first + i : first + i + 1], x.shape)

    for k in range(0, count, group):
        small = {(a, b): lane(rows[k + a], k + b) for a in range(group) for b in range(a, group)}
        for a in range(group):
            root = lax.rsqrt(small[a, a])
            upper = {b: small[a, b] * root for b in range(a + 1, group)}
            rows[k + a] = rows[k + a] * root
            for c in range(a + 1, group):
                rows[k + c] = rows[k + c] - upper[c] * rows[k + a]
                for b in range(c, group):
                    small[c, b] = small[c, b] - upper[c] * upper[b]
        for i in range(k + group, count):
            for a in range(group):
                rows[i] = rows[i] - lane(rows[k + a], i) * rows[k + a]
    return rows


def whole(
    list_ref, count_ref, loc_ref, state_ref, obs_hbm, prec_hbm, innov_hbm, prior_hbm,
    out_ref,
    listed, seen_obs, table, states_in, wide, result, seen, entry_rows, picked_rows, given_rows, extra, system, diag, vectors, qcol,
    ring_send, ring_recv, obs_send, obs_recv, state_send, state_recv, out_send, out_recv, own_sem,
    table_send, table_recv, load_sem, obs_ref, given_ref, prior_ref,
    *blocks, side, nb, sub, group,
):
    pieces, mems, entries, part, width = seen_obs.shape
    members_dev, count = obs_ref.shape[:2]
    slots, rows_space = list_ref.shape
    regions = rows_space // mems
    members = mems * members_dev
    p_size = state_ref.shape[2]
    half = count // 2
    space, mem = lax.axis_index("space"), lax.axis_index("mem")
    core = mem % 2
    x, z = space // side, space % side
    first = mem * regions

    def at(axis, i, j):
        dx, dz = (i, j) if axis == 0 else (j, i)
        return (x + dx + side) % side * side + (z + dz + side) % side

    def peer(step):
        return (mem // 2 + step // 2) % (mems // 2) * 2 + (core + step % 2) % 2

    loads = [
        pltpu.make_async_copy(obs_hbm, obs_ref, load_sem.at[0]),
        pltpu.make_async_copy(prec_hbm, given_ref.at[0], load_sem.at[1]),
        pltpu.make_async_copy(innov_hbm, given_ref.at[1], load_sem.at[2]),
        pltpu.make_async_copy(prior_hbm, prior_ref, load_sem.at[3]),
    ]
    for load in loads:
        load.start()
    barrier = pltpu.get_barrier_semaphore()
    for there in [at(0, 1, 0), at(0, -1, 0), at(0, 0, 1), at(0, 0, -1)]:
        pl.semaphore_signal(barrier, inc=1, device_id={"space": there, "mem": mem})
    for step in range(1, mems):
        pl.semaphore_signal(barrier, inc=1, device_id={"space": space, "mem": peer(step)})

    def turn(p):
        for k in range(part):
            wide[0, k * count : (k + 1) * count, :] = obs_ref[p * part + k].astype(F32)

        def one(b, carry):
            block = wide[0, pl.ds(b, part, stride=count), :].astype(BF16)
            blocks[p][space * count + b] = block
            return carry

        lax.fori_loop(0, count, one, 0, unroll=8)

    loads[0].wait()
    turn(0)
    pl.semaphore_wait(barrier, 4 + mems - 1)

    rings = [*blocks, table]

    def send(p, axis, number, chunk, share, to):
        start, size = {"all": (0, half), "low": (0, half // 2), "high": (half // 2, half // 2)}[share]
        rows = pl.ds(pl.multiple_of(chunk * count + start + axis * half, size), size)
        return pltpu.make_async_remote_copy(
            src_ref=rings[p].at[rows],
            dst_ref=rings[p].at[rows],
            send_sem=ring_send.at[p, axis, number],
            recv_sem=ring_recv.at[p, axis, number],
            device_id={"space": to, "mem": mem},
        )

    order = (0, -1, 1, 2)

    def copy_of(p, axis, number):
        if number == 0:
            return send(p, axis, 0, at(axis, 0, 0), "all", at(axis, 1, 0))
        if number == 1:
            return send(p, axis, 1, at(axis, 0, 0), "all", at(axis, -1, 0))
        if number == 2:
            return send(p, axis, 2, at(axis, -1, 0), "low", at(axis, 1, 0))
        if number == 3:
            return send(p, axis, 3, at(axis, 1, 0), "high", at(axis, -1, 0))
        d, kind = order[(number - 4) // 4], (number - 4) % 4
        if kind == 0:
            return send(p, axis, number, at(axis, d, 0), "all", at(axis, 0, 1))
        if kind == 1:
            return send(p, axis, number, at(axis, d, 0), "all", at(axis, 0, -1))
        if kind == 2:
            return send(p, axis, number, at(axis, d, -1), "low", at(axis, 0, 1))
        return send(p, axis, number, at(axis, d, 1), "high", at(axis, 0, -1))

    sent = []

    def start(p, *numbers):
        for number in numbers:
            for axis in (0, 1):
                copy = copy_of(p, axis, number)
                copy.start()
                sent.append(copy)

    def arrive(p, *numbers):
        for number in numbers:
            for axis in (0, 1):
                copy_of(p, axis, number).wait_recv()

    def begin(p):
        start(p, 0, 1, 4, 5)

    def spread(p):
        arrive(p, 0)
        start(p, 2, 8, 9)
        arrive(p, 1)
        start(p, 3, 12, 13)
        arrive(p, 2, 3)
        start(p, 16, 17)

    def hand_on(p):
        for j in range(4):
            for kind in (0, 1):
                arrive(p, 4 + 4 * j + kind)
                start(p, 4 + 4 * j + kind + 2)

    def gathered(p):
        for j in range(4):
            arrive(p, 6 + 4 * j, 7 + 4 * j)

    def state_copy(step):
        to = peer(step)
        return pltpu.make_async_remote_copy(
            src_ref=state_ref.at[:, pl.ds(pl.multiple_of(to * regions, regions), regions), :],
            dst_ref=states_in.at[mem],
            send_sem=state_send.at[step],
            recv_sem=state_recv.at[step],
            device_id={"space": space, "mem": to},
        )

    def obs_copy(p, step):
        to = peer(step)
        return pltpu.make_async_remote_copy(
            src_ref=listed.at[p, pl.ds(pl.multiple_of(to * entries, entries), entries)],
            dst_ref=seen_obs.at[p, mem],
            send_sem=obs_send.at[p, step],
            recv_sem=obs_recv.at[p, step],
            device_id={"space": space, "mem": to},
        )

    local = []

    def begin_states():
        copy = pltpu.make_async_copy(
            state_ref.at[:, pl.ds(pl.multiple_of(first, regions), regions), :],
            states_in.at[mem],
            own_sem.at[pieces],
        )
        copy.start()
        local.append(copy)
        for step in range(1, mems):
            state_copy(step).start()

    begin(0)
    begin_states()
    local_states = local.pop()
    for p in range(1, pieces):
        turn(p)
    for load in loads[1:]:
        load.wait()
    here = pl.ds(pl.multiple_of(space * count, count), count)
    table[here, :] = jnp.where(core == 0, given_ref[0], given_ref[1])
    spread(0)
    begin(1)
    for p in range(pieces):
        hand_on(p)
        if p + 1 < pieces:
            spread(p + 1)
        if p + 1 < pieces:
            begin(p + 2 if p + 2 < pieces else pieces)
        else:
            spread(pieces)
        gathered(p)

        for step in sorted(range(mems), key=lambda k: (k == 0, k == 1, k // 2 != mems // 4)):
            to = peer(step)

            def pick(r, carry, p=p, to=to):
                row = to * regions + r
                for l in range(slots):
                    listed[p, row * slots + l] = blocks[p][list_ref[l, row]]
                return carry

            lax.fori_loop(0, regions, pick, 0, unroll=4)
            if step:
                obs_copy(p, step).start()
        mine = pltpu.make_async_copy(
            listed.at[p, pl.ds(pl.multiple_of(mem * entries, entries), entries)],
            seen_obs.at[p, mem],
            own_sem.at[p],
        )
        mine.start()
        local.append(mine)

    extra[...] = jnp.zeros_like(extra)
    shares_all = prior_ref[pl.ds(pl.multiple_of(first, regions), regions), :]
    shares_all = shares_all / jnp.sum(shares_all, axis=1, keepdims=True)
    root_t = jnp.transpose(jnp.sqrt(members * shares_all))
    for r in range(regions):
        qcol[r] = jnp.broadcast_to(root_t[:, r : r + 1], (members, 128))
    halves = members // 128
    hand_on(pieces)
    gathered(pieces)
    def pick_rows(r, carry):
        for c in range(2):
            for l in range(slots):
                block = list_ref[l, (mem - core + c) * regions + r]
                picked_rows[c, pl.ds(r * slots + l, 1), :] = table[pl.ds(block, 1), :]
        return carry

    lax.fori_loop(0, regions, pick_rows, 0, unroll=2)
    other = pltpu.make_async_remote_copy(
        src_ref=picked_rows.at[1 - core],
        dst_ref=given_rows.at[core],
        send_sem=table_send,
        recv_sem=table_recv,
        device_id={"space": space, "mem": mem + 1 - 2 * core},
    )
    other.start()
    given_rows[core] = picked_rows[core]
    other.wait()

    def fetch(r, carry):
        row = first + r
        for l in range(slots):
            at_e = pl.ds(r * slots + l, 1)
            live = jnp.where(l < count_ref[row], loc_ref[l, row], 0.0)
            entry_rows[0, at_e, :] = live * given_rows[0, at_e, :]
        return carry

    lax.fori_loop(0, regions, fetch, 0)
    entry_rows[0] = jnp.sqrt(entry_rows[0])
    entry_rows[1] = entry_rows[0] * given_rows[1]
    for copy in sent:
        copy.wait_send()
    for p in range(0, pieces, 2):
        for which in (p, p + 1):
            local[which].wait()
            for step in range(1, mems):
                obs_copy(which, step).wait()

        def weigh(r, carry, p=p):
            for l in range(slots):
                scale = entry_rows[0, pl.ds(r * slots + l, 1), :]
                for m in range(mems):
                    picked = jnp.concatenate(
                        [seen_obs[p, m, r * slots + l], seen_obs[p + 1, m, r * slots + l]], axis=0
                    ).astype(F32)
                    at_m = slice(m * members_dev + p * part, m * members_dev + (p + 2) * part)
                    seen[r, at_m, l * width : (l + 1) * width] = (picked * scale).astype(BF16)
            return carry

        if p + 2 < pieces:
            lax.fori_loop(0, regions, weigh, 0, unroll=2)

    row_id = lax.broadcasted_iota(jnp.int32, (members, members), 0)
    col_id = lax.broadcasted_iota(jnp.int32, (members, members), 1)

    def shares_of(r):
        s = prior_ref[pl.ds(first + r, 1), :]
        return s / jnp.sum(s, axis=1, keepdims=True)

    def build(r, carry):
        weigh(r, carry)
        for l in range(slots):
            cols = slice(l * width, (l + 1) * width)
            high, low = split(entry_rows[1, pl.ds(r * slots + l, 1), :])
            extra[0:1, cols] = high.astype(F32)
            extra[1:2, cols] = low.astype(F32)
        all_seen = seen[r]
        gram = dot(all_seen, all_seen, ((1,), (1,)))
        proj = dot(extra[...].astype(BF16), all_seen, ((1,), (1,)))
        proj = proj[0:1] + proj[1:2]
        shares = shares_of(r)
        root = jnp.sqrt(members * shares)
        left = dot(jnp.broadcast_to(shares, (8, members)), gram, ((1,), (0,)), HIGHEST)[0:1]
        centred = gram - left
        centred = centred - jnp.sum(centred * shares, axis=1, keepdims=True)
        q = jnp.concatenate([qcol[r]] * halves, axis=1)
        full = q * centred * root + jnp.where(row_id == col_id, (members - 1) / INFLATION, 0.0)
        at_r = pl.ds(pl.multiple_of(r * members, members), members)
        for h in range(halves):
            system[h, at_r, :] = full[:, h * 128 : (h + 1) * 128]
        vectors[pl.ds(r, 1), :] = root * (proj - jnp.sum(shares * proj, axis=1, keepdims=True))
        return carry

    lax.fori_loop(0, regions, build, 0, unroll=True)

    def take_states():
        for step in range(1, mems):
            state_copy(step).wait()
        local_states.wait()
        for m in range(mems):
            many = states_in[m].astype(F32).reshape(members_dev * regions, p_size)
            for h in range(p_size // 128):
                wide[h, m * members_dev * regions : (m + 1) * members_dev * regions, :] = many[
                    :, h * 128 : (h + 1) * 128
                ]

    lane_id = lax.broadcasted_iota(jnp.int32, (regions, 128), 1)
    for b in range(members // nb):
        h_b, place = b * nb // 128, b * nb % 128
        if b == members // nb // 2:
            take_states()
        for part_b in range(0, nb, sub):
            if part_b == 0:
                rows = []
                for i in range(sub):
                    row = system[h_b, pl.ds(b * nb + i, regions, stride=members), :]
                    if place:
                        row = pltpu.roll(row, 128 - place, 1)
                    rows.append(jnp.where(lane_id < nb, row, jnp.where(lane_id == nb + i, 1.0, 0.0)))
            else:
                rows = [diag[pl.ds(part_b + i, regions, stride=nb), :] for i in range(sub)]
            rows = eliminate(rows, group, part_b)
            for i in range(sub):
                diag[pl.ds(part_b + i, regions, stride=nb), :] = rows[i]
            if part_b:
                continue
            for r in range(regions):
                ready = diag[r * nb : r * nb + sub, :]
                later = system[h_b, r * members + b * nb + sub : r * members + (b + 1) * nb, :]
                if place:
                    later = pltpu.roll(later, 128 - place, 1)
                lanes = lax.broadcasted_iota(jnp.int32, (nb - sub, 128), 1)
                which = lax.broadcasted_iota(jnp.int32, (nb - sub, 128), 0)
                later = jnp.where(lanes < nb, later, jnp.where(lanes == nb + sub + which, 1.0, 0.0))
                later = later - dot(ready[:, sub:nb], ready, ((0,), (0,)), HIGHEST)
                diag[r * nb + sub : (r + 1) * nb, :] = later

        def sweep(r, carry, b=b, h_b=h_b, place=place):
            begins = r * members + b * nb
            band_rows = pl.ds(pl.multiple_of(begins, nb), nb)
            small = diag[pl.ds(pl.multiple_of(r * nb, nb), nb), :][:, nb : 2 * nb]
            band = jnp.concatenate([system[h, band_rows, :] for h in range(halves)], axis=1)
            ids = lax.broadcasted_iota(jnp.int32, (nb, members), 1)
            rid = lax.broadcasted_iota(jnp.int32, (nb, members), 0)
            mine = (ids >= b * nb) & (ids < (b + 1) * nb)
            band = jnp.where(mine, jnp.where(ids - b * nb == rid, 1.0, 0.0), band)
            done = dot(small, band, ((1,), (0,)), HIGHEST)
            kept = jnp.where(ids < (b + 1) * nb, done, 0.0)
            for h in range(halves):
                system[h, band_rows, :] = kept[:, h * 128 : (h + 1) * 128]
            rest = members - (b + 1) * nb
            if rest:
                below = pl.ds(pl.multiple_of(begins + nb, nb), rest)
                change = dot(done[:, (b + 1) * nb :], done, ((0,), (0,)), HIGHEST)
                for h in range(halves):
                    old = system[h, below, :]
                    if h == h_b:
                        lanes = lax.broadcasted_iota(jnp.int32, (rest, 128), 1)
                        old = jnp.where((lanes >= place) & (lanes < place + nb), 0.0, old)
                    system[h, below, :] = old - change[:, h * 128 : (h + 1) * 128]
            return carry

        lax.fori_loop(0, regions, sweep, 0, unroll=True)

    def out_copy(r, step):
        to = peer(step)
        return pltpu.make_async_remote_copy(
            src_ref=result.at[r, pl.ds(pl.multiple_of(to * members_dev, members_dev), members_dev), :],
            dst_ref=out_ref.at[first + r],
            send_sem=out_send.at[r, step],
            recv_sem=out_recv.at[r, step],
            device_id={"space": space, "mem": to},
        )

    def own_out(r):
        return pltpu.make_async_copy(
            result.at[r, pl.ds(pl.multiple_of(mem * members_dev, members_dev), members_dev), :],
            out_ref.at[first + r],
            out_send.at[r, 0],
        )

    def finish(r, carry):
        at_r = pl.ds(pl.multiple_of(r * members, members), members)
        inverse = jnp.concatenate([system[h, at_r, :] for h in range(halves)], axis=1)
        shares = shares_of(r)
        root = jnp.sqrt(members * shares)
        solved = jnp.sum(inverse * vectors[pl.ds(r, 1), :], axis=1, keepdims=True)
        weights = jnp.sum(inverse * solved, axis=0, keepdims=True)
        mixing = root * (weights + math.sqrt(members - 1.0) * inverse)
        mixing = mixing - jnp.sum(mixing, axis=1, keepdims=True) * shares + shares
        high, low = split(mixing)
        states = jnp.concatenate(
            [wide[h, pl.ds(r, members, stride=regions), :] for h in range(p_size // 128)], axis=1
        ).astype(BF16)
        done = dot(high, states, ((1,), (0,))) + dot(low, states, ((1,), (0,)))
        result[r] = done.astype(BF16)
        own_out(r).start()
        for step in range(1, mems):
            out_copy(r, step).start()
        return carry

    lax.fori_loop(0, regions, finish, 0, unroll=4)

    def close(r, carry):
        own_out(r).wait()
        for step in range(1, mems):
            out_copy(r, step).wait()
        return carry

    lax.fori_loop(0, regions, close, 0)


SMEM = pl.BlockSpec(memory_space=pltpu.SMEM)
VMEM = pl.BlockSpec(memory_space=pltpu.VMEM)
HBM = pl.BlockSpec(memory_space=pltpu.HBM)


def body(
    ensemble_state, obs_ens, innovation, obs_prec, block_list, block_count, loc_weight, prior_weight
):
    spaces, mems = lax.axis_size("space"), lax.axis_size("mem")
    members_dev, regions_dev, p_size = ensemble_state.shape
    blocks_dev, width = obs_ens.shape[1:]
    slots = block_list.shape[1]
    regions = regions_dev // mems
    entries = regions * slots
    members = members_dev * mems
    pieces = 4
    part = members_dev // pieces
    nb = 64
    dma = pltpu.SemaphoreType.DMA
    updated = pl.pallas_call(
        functools.partial(whole, side=math.isqrt(spaces), nb=nb, sub=32, group=8),
        in_specs=[SMEM, SMEM, SMEM, HBM, HBM, HBM, HBM, HBM],
        out_specs=VMEM,
        out_shape=jax.ShapeDtypeStruct((regions_dev, members_dev, p_size), BF16),
        scratch_shapes=[
            pltpu.VMEM((pieces, regions_dev * slots, part, width), BF16),
            pltpu.VMEM((pieces, mems, entries, part, width), BF16),
            pltpu.VMEM((blocks_dev * spaces, width), F32),
            pltpu.VMEM((mems, members_dev, regions, p_size), BF16),
            pltpu.VMEM((p_size // 128, max(members * regions, members_dev * blocks_dev), 128), F32),
            pltpu.VMEM((regions, members, p_size), BF16),
            pltpu.VMEM((regions, members, slots * width), BF16),
            pltpu.VMEM((2, entries, width), F32),
            pltpu.VMEM((2, entries, width), F32),
            pltpu.VMEM((2, entries, width), F32),
            pltpu.VMEM((16, slots * width), F32),
            pltpu.VMEM((members // 128, regions * members, 128), F32),
            pltpu.VMEM((regions * nb, 128), F32),
            pltpu.VMEM((regions, members), F32),
            pltpu.VMEM((regions, members, 128), F32),
            dma((pieces + 1, 2, 20)),
            dma((pieces + 1, 2, 20)),
            dma((pieces, mems)),
            dma((pieces, mems)),
            dma((mems,)),
            dma((mems,)),
            dma((regions, mems)),
            dma((regions, mems)),
            dma((pieces + 1,)),
            dma(()),
            dma(()),
            dma((4,)),
            pltpu.VMEM((members_dev, blocks_dev, width), BF16),
            pltpu.VMEM((2, blocks_dev, width), F32),
            pltpu.VMEM((regions_dev, members), F32),
            *[pltpu.VMEM((blocks_dev * spaces, part, width), BF16) for _ in range(pieces)],
        ],
        compiler_params=pltpu.CompilerParams(
            vmem_limit_bytes=63 << 20, collective_id=0, has_side_effects=True
        ),
    )(
        block_list.T, block_count, loc_weight.T,
        ensemble_state, obs_ens, obs_prec, innovation, prior_weight,
    )
    return jnp.transpose(updated, (1, 0, 2))


def solution(mesh):
    return jax.shard_map(
        body,
        mesh=mesh,
        in_specs=(
            P("mem", "space", None),
            P("mem", "space", None),
            P("space", None),
            P("space", None),
            P("space", None),
            P("space"),
            P("space", None),
            P("space", None),
        ),
        out_specs=P("mem", "space", None),
        check_vma=False,
    )
```
